256 devices in a mesh: space: 32 (over y, z), chan: 8 (over x, core).
Axes of the slice: x: 4, y: 4, z: 8, core: 2. Of those that a mesh axis runs over, the one named last changes fastest.
Arguments:
- features: bfloat16 [65536, 256], P('space', 'chan'), may hold values from -6 to 6
- kernel_map: int32 [32, 27, 16, 3], P('space'), may hold values from 0 to 31, as said below
- block_count: int32 [32], replicated, may hold values from 3 to 16, as said below
- weight_one: bfloat16 [27, 256, 256], P(None, 'chan'), may hold values from -0.078125 to 0.078125
- weight_two: bfloat16 [27, 256, 256], P(None, 'chan'), may hold values from -0.078125 to 0.078125
- cotangent: bfloat16 [65536, 256], P('space', 'chan'), may hold values from -0.026977539 to 0.026977539
Outputs:
- output: bfloat16 [65536, 256], P('space', 'chan')
- grad_one: float32 [27, 256, 256], P(None, 'chan', 'space')
- grad_two: float32 [27, 256, 256], P(None, 'chan', 'space')
The draws below stay inside these ranges and needn't reach their ends.
Inputs may be any that keep to these rules, and one draw needn't show every extreme that they name: `kernel_map`: column 0 of slab s's entries is s - 1, s or s + 1. Column 1 is a block below block_count of that source slab; from slab s - 1 it is one of that slab's last 2 live blocks, from slab s + 1 one of its first 2. Column 2 lies below 16. Entries stand in offset order, 16 per offset and slab. `block_count`: at least one slab has all 16 blocks live.
All inputs are finite; a program needn't handle non-finite values.
Results may differ from the reference program's by a relative error of at most 0.015.
Values may be sent and summed in bfloat16 or wider, within the bound.
A program may use at most 64 MiB of HBM per device.

```python
import jax
import jax.numpy as jnp
from jax import lax

C = 256
KVOL = 27
BLK = 128
HB = 2
BLK_DEV = 16
EPK = 16
ROWS = 65536
N_SPACE = 32


def shared_counts(key):
    inner = jax.random.fold_in(key, 7)
    key_a, key_b, key_c = jax.random.split(inner, 3)
    lowest = HB + 1
    spread = BLK_DEV - lowest
    first = jax.random.randint(key_a, (N_SPACE,), 0, spread + 1)
    second = jax.random.randint(key_b, (N_SPACE,), 0, spread + 1)
    counts = lowest + first * second // spread
    fullest = jax.random.randint(key_c, (), 0, N_SPACE)
    return jnp.where(jnp.arange(N_SPACE) == fullest, BLK_DEV, counts).astype(jnp.int32)


def draw_block_count(key, part):
    return shared_counts(key)


def draw_kernel_map(key, part):
    counts = shared_counts(key)
    inner = jax.random.fold_in(key, 11)
    key_a, key_b, key_c = jax.random.split(inner, 3)
    shape = (N_SPACE, KVOL, EPK)
    shard = jnp.broadcast_to(jnp.arange(N_SPACE, dtype=jnp.int32)[:, None, None], shape)
    pick = jax.random.randint(key_a, shape, 0, 8)
    offset = jnp.where(pick == 0, -1, jnp.where(pick == 1, 1, 0))
    source = jnp.clip(shard + offset, 0, N_SPACE - 1)
    source_count = counts[source]
    fraction = jax.random.randint(key_b, shape, 0, 1048576)
    same_block = fraction * source_count // 1048576
    rim_block = fraction * HB // 1048576
    block = jnp.where(source == shard, same_block, jnp.where(source < shard, source_count - HB + rim_block, rim_block))
    target = jax.random.randint(key_c, shape, 0, BLK_DEV)
    return jnp.stack([source, block, target], -1).astype(jnp.int32)


def level_of(key, shape, shards, least, top_value):
    loudness, own = 1.0, jax.random.fold_in(key, 6)
    for position, blocks in shards:
        heights = jnp.exp(jax.random.uniform(jax.random.fold_in(own, position), (blocks,), jnp.float32, least / len(shards), top_value / len(shards)))
        loudness = loudness * jnp.repeat(heights, shape[position] // blocks).reshape([-1 if axis == position else 1 for axis in range(len(shape))])
    return loudness


def scatter_about(stream_key, extent, scale, most, pieces=(), kind=jnp.bfloat16):
    array = scale * jax.random.normal(stream_key, extent, jnp.float32)
    if pieces:
        array = array * level_of(stream_key, extent, pieces, -0.22, 0.18)
    return jnp.clip(array, -most, most).astype(kind)


def setup_inputs(seed: int = 0) -> dict:
    splits = jax.random.split(jax.random.key(seed), 7)
    features = scatter_about(splits[0], (ROWS, C), 1.0, 6.0, ((0, 32), (1, 8)))
    kernel_map = draw_kernel_map(jax.random.fold_in(splits[6], 71), 0)
    block_count = draw_block_count(jax.random.fold_in(splits[6], 71), 0)
    weight_one = scatter_about(splits[3], (KVOL, C, C), (C * KVOL * EPK // BLK_DEV) ** -0.5, 0.078125, ((1, 8),))
    weight_two = scatter_about(splits[4], (KVOL, C, C), (C * KVOL * EPK // BLK_DEV) ** -0.5, 0.078125, ((1, 8),))
    cotangent = scatter_about(splits[5], (ROWS, C), 0.0045, 0.026977539, ((0, 32), (1, 8)))
    return {"features": features, "kernel_map": kernel_map, "block_count": block_count, "weight_one": weight_one, "weight_two": weight_two, "cotangent": cotangent}


def entry_tables(kernel_map, block_count, shard):
    entry = kernel_map[shard]
    source = (entry[..., 0] * BLK_DEV + entry[..., 1]).astype(jnp.int32)
    live = entry[..., 2] < block_count[shard]
    choose = ((entry[..., 2][..., None] == jnp.arange(BLK_DEV, dtype=jnp.int32)) & live[..., None]).astype(jnp.float32)
    return source, choose


def convolve(feat, weights, kernel_map, block_count):
    blocks = feat.reshape(N_SPACE * BLK_DEV, BLK, C)
    kernel = weights.astype(jnp.float32)

    def one(shard):
        source, choose = entry_tables(kernel_map, block_count, shard)
        picked = blocks[source].astype(jnp.float32)
        prod = jnp.einsum("kerc,kdc->kerd", picked, kernel)
        return jnp.einsum("keb,kerd->brd", choose, prod)

    out = lax.map(one, jnp.arange(N_SPACE, dtype=jnp.int32))
    return out.reshape(ROWS, C)


def backward_pass(feat, grads, weights, kernel_map, block_count, want_input):
    blocks = feat.reshape(N_SPACE * BLK_DEV, BLK, C)
    grad_blocks = grads.astype(jnp.float32).reshape(N_SPACE, BLK_DEV, BLK, C)
    kernel = weights.astype(jnp.float32)

    def step(carry, shard):
        wsum, isum = carry
        source, choose = entry_tables(kernel_map, block_count, shard)
        picked = blocks[source].astype(jnp.float32)
        chosen = jnp.einsum("keb,brd->kerd", choose, grad_blocks[shard])
        wsum = wsum + jnp.einsum("kerc,kerd->kdc", picked, chosen)
        if want_input:
            contrib = jnp.einsum("kerd,kdc->kerc", chosen, kernel)
            isum = isum.at[source.reshape(-1)].add(contrib.reshape(-1, BLK, C))
        return (wsum, isum), None

    init_w = jnp.zeros((KVOL, C, C), jnp.float32)
    if want_input:
        init_i = jnp.zeros((N_SPACE * BLK_DEV, BLK, C), jnp.float32)
    else:
        init_i = jnp.zeros((1,), jnp.float32)
    (wsum, isum), _ = lax.scan(step, (init_w, init_i), jnp.arange(N_SPACE, dtype=jnp.int32))
    return wsum, isum


def reference(features, kernel_map, block_count, weight_one, weight_two, cotangent):
    z_one = convolve(features, weight_one, kernel_map, block_count)
    hidden = jax.nn.silu(z_one).astype(jnp.bfloat16)
    output = convolve(hidden, weight_two, kernel_map, block_count).astype(jnp.bfloat16)
    grad_two, grad_hidden = backward_pass(hidden, cotangent, weight_two, kernel_map, block_count, True)
    grad_hidden = grad_hidden.reshape(ROWS, C)
    gate = jax.nn.sigmoid(z_one)
    grad_z = (grad_hidden * gate * (1.0 + z_one * (1.0 - gate))).astype(jnp.bfloat16)
    grad_one, _ = backward_pass(features, grad_z, weight_one, kernel_map, block_count, False)
    return output, grad_one, grad_two
```

```python
import functools

import jax
import jax.numpy as jnp
from jax import lax
from jax.experimental import pallas as pl
from jax.experimental.pallas import tpu as pltpu
from jax.sharding import PartitionSpec as P

MESH = pl.DeviceIdType.MESH
C = 256
K = 27
BLK = 128
HB = 2
NB = 16
EPK = 16
NX = NB + 2 * HB
NE = K * EPK
NCHAN = 8
NSPACE = 32
D = C // NCHAN
CH = C // NSPACE
KD = K * D
KP = 1024
OWN = NB * BLK
RIM = HB * BLK
EXT = NX * BLK
NSLOT = K * NX
F32 = jnp.float32
BF16 = jnp.bfloat16

T_ROWS = 0
T_SLOTS = NE
T_TEND = 2 * NE
T_SEND = T_TEND + NB
T_LAST = T_SEND + NSLOT


def nt(a, b):
    return lax.dot_general(a, b, (((1,), (1,)), ((), ())), preferred_element_type=F32)


def eye(n):
    row = lax.broadcasted_iota(jnp.int32, (n, n), 0)
    col = lax.broadcasted_iota(jnp.int32, (n, n), 1)
    return jnp.where(row == col, 1.0, 0.0).astype(BF16)


def tables(kernel_map, block_count):
    shard = lax.axis_index("space")
    own = block_count[shard]
    left = block_count[jnp.maximum(shard - 1, 0)]
    entries = kernel_map[0].reshape(NE, 3)
    source, inblock, target = entries[:, 0], entries[:, 1], entries[:, 2]
    pos = jnp.where(
        source == shard,
        inblock,
        jnp.where(source < shard, NB + inblock - (left - HB), NB + HB + inblock),
    )
    live = target < own
    number = jnp.arange(NE, dtype=jnp.int32)
    offset = number // EPK

    def by(key, payload, bits, ends):
        full = key * 512 + number
        rank = jnp.sum((full[None, :] < full[:, None]).astype(jnp.int32), 1)
        value = key * bits + payload
        order = jnp.sum(jnp.where(rank[None, :] == number[:, None], value[None, :], 0), 1)
        keys = order // bits
        same = jnp.concatenate([jnp.zeros((1,), jnp.int32), (keys[1:] == keys[:-1]).astype(jnp.int32)])
        at = jnp.arange(ends, dtype=jnp.int32)[:, None]
        upto = jnp.sum((key[None, :] <= at).astype(jnp.int32), 1)
        there = jnp.sum((key[None, :] == at).astype(jnp.int32), 1)
        return (order % bits, same), (jnp.maximum(upto - 1, 0), (there > 0).astype(jnp.int32))

    rows, tend = by(jnp.where(live, target, NB), pos * K + offset, 1024, NB)
    slots, send = by(jnp.where(live, offset * NX + pos, NSLOT), target, 32, NSLOT)
    last = own - HB + jnp.arange(HB, dtype=jnp.int32)
    which = (last[:, None] == jnp.arange(NB, dtype=jnp.int32)).astype(jnp.int32).reshape(-1)
    index = jnp.concatenate([rows[0], slots[0], tend[0], send[0], last])
    factor = jnp.concatenate([rows[1], slots[1], tend[1], send[1], which])
    return index, factor.astype(F32)


def kernel(
    tab, fac, x_ref, g_ref, w1_ref, w2_ref,
    out_ref, g1_ref, g2_ref,
    xe, he, xrim, hrim, xall, hall, w2t, gblk, zblk, zall, y, run, a_g, a_z, part, got, ghown,
    rimx, rimh, back_out, back_in, gsend1, gsend2, grecv1, grecv2,
    xs, xr, rs, rr, hs, hr, qs, qr, ps, pr, ns, nr, s1s, s1r, s2s, s2r,
):
    chan = lax.axis_index("chan")
    space = lax.axis_index("space")
    right = lax.rem(space + 1, NSPACE)
    left = lax.rem(space + NSPACE - 1, NSPACE)

    barrier = pltpu.get_barrier_semaphore()
    for j in range(1, NCHAN):
        pl.semaphore_signal(
            barrier, inc=1, device_id=(space, lax.rem(chan + j, NCHAN)), device_id_type=MESH
        )

    @pl.loop(1, NSPACE)
    def _(j):
        pl.semaphore_signal(
            barrier, inc=1, device_id=(lax.rem(space + j, NSPACE), chan), device_id_type=MESH
        )

    def remote(src, dst, ssem, rsem, device):
        return pltpu.make_async_remote_copy(
            src_ref=src, dst_ref=dst, send_sem=ssem, recv_sem=rsem, device_id=device, device_id_type=MESH
        )

    mine = pl.ds(pl.multiple_of(chan * D, D), D)

    def gather_copies(own, whole, lanes, ssem, rsem, first):
        return [
            remote(
                own, whole.at[mine, lanes], ssem.at[first + j - 1], rsem.at[first + j - 1],
                (space, lax.rem(chan + j, NCHAN)),
            )
            for j in range(1, NCHAN)
        ]

    def rim_copies(own, last, rim, ssem, rsem):
        return [
            remote(last, rim.at[:, pl.ds(0, RIM)], ssem.at[0], rsem.at[0], (right, chan)),
            remote(own.at[:, pl.ds(0, RIM)], rim.at[:, pl.ds(RIM, RIM)], ssem.at[1], rsem.at[1], (left, chan)),
        ]

    def load_rim(blocks, last):
        for u in range(HB):
            last[:, u * BLK : (u + 1) * BLK] = blocks[tab[T_LAST + u]].astype(BF16)

    body = pl.ds(0, OWN)
    rims = pl.ds(OWN, 2 * RIM)

    ident = eye(D)
    for b in range(0, NB, 4):
        four = nt(ident, x_ref[b * BLK : (b + 4) * BLK, :])
        xe[:, b * BLK : (b + 4) * BLK] = four.astype(BF16)
        for u in range(4):
            gblk[b + u] = four[:, u * BLK : (u + 1) * BLK]
    load_rim(gblk, rimx)

    pl.semaphore_wait(barrier, NCHAN - 1 + NSPACE - 1)

    x_rims = rim_copies(xe, rimx, xrim, rs, rr)
    for copy in x_rims:
        copy.start()
    x_bodies = gather_copies(xe, xall, body, xs, xr, 0)
    for copy in x_bodies:
        copy.start()
    xall[mine, body] = xe[...]

    def scan(src, base):
        def step(i, total):
            for u in range(8):
                n = i * 8 + u
                total = total * fac[base + n] + src[tab[base + n]]
                run[n] = total
            return total

        lax.fori_loop(0, NE // 8, step, jnp.zeros((D, BLK), F32))

    def run_end(at):
        return run[tab[at]] * fac[at]

    def fill_slots(dst):
        @pl.loop(0, K)
        def _(k):
            at = pl.ds(pl.multiple_of(k * D, D), D)
            for p in range(NX):
                dst[at, p * BLK : (p + 1) * BLK] = run_end(T_SEND + k * NX + p).astype(BF16)

    for b in range(0, NB, 4):
        four = nt(ident, g_ref[b * BLK : (b + 4) * BLK, :])
        for u in range(4):
            gblk[b + u] = four[:, u * BLK : (u + 1) * BLK]
    a_g[KD:, :] = jnp.zeros((KP - KD, EXT), BF16)
    a_z[KD:, :] = jnp.zeros((KP - KD, EXT), BF16)
    w2t[:, KD:] = jnp.zeros((C, KP - KD), BF16)
    w2t[:, :KD] = nt(eye(C), w2_ref[...]).astype(BF16)
    scan(gblk, T_SLOTS)
    fill_slots(a_g)

    for copy in x_rims:
        copy.wait_recv()
    x_sides = gather_copies(xrim, xall, rims, xs, xr, NCHAN - 1)
    for copy in x_sides:
        copy.start()
    xall[mine, rims] = xrim[...]

    @pl.loop(0, NX // 2)
    def _(p):
        two = pl.ds(pl.multiple_of(p * 2 * BLK, 2 * BLK), 2 * BLK)
        part[:, two] = jnp.dot(w2t[...], a_g[:, two], preferred_element_type=F32).astype(BF16)

    p_copies = []
    for j in range(1, NCHAN):
        to = lax.rem(chan + j, NCHAN)
        p_copies.append(
            remote(
                part.at[pl.ds(pl.multiple_of(to * D, D), D), :], got.at[j - 1],
                ps.at[j - 1], pr.at[j - 1], (space, to),
            )
        )
    for copy in p_copies:
        copy.start()

    def products(w_ref, whole):
        @pl.loop(0, NX // 2)
        def _(p):
            two = pl.ds(pl.multiple_of(p * 2 * BLK, 2 * BLK), 2 * BLK)
            prod = jnp.dot(w_ref[...], whole[:, two], preferred_element_type=F32)
            y[pl.ds(p * 2 * K, K)] = prod[:, :BLK].reshape(K, D, BLK)
            y[pl.ds(p * 2 * K + K, K)] = prod[:, BLK:].reshape(K, D, BLK)

    for copy in x_bodies + x_sides:
        copy.wait_recv()
    products(w1_ref, xall)
    scan(y, T_ROWS)
    for b in range(NB):
        z = run_end(T_TEND + b)
        zblk[b] = z
        h = z / (1.0 + jnp.exp(-z))
        gblk[b] = h
        he[:, b * BLK : (b + 1) * BLK] = h.astype(BF16)
    load_rim(gblk, rimh)
    h_rims = rim_copies(he, rimh, hrim, qs, qr)
    for copy in h_rims:
        copy.start()
    h_bodies = gather_copies(he, hall, body, hs, hr, 0)
    for copy in h_bodies:
        copy.start()
    hall[mine, body] = he[...]

    for copy in p_copies:
        copy.wait_recv()
    for p in range(0, NX, 4):
        at = pl.ds(p * BLK, 4 * BLK)
        total = part[mine, at].astype(F32)
        for j in range(NCHAN - 1):
            total = total + got[j, :, at].astype(F32)
        ghown[:, at] = total
    back_out[0] = ghown[:, OWN : OWN + RIM]
    back_out[1] = ghown[:, OWN + RIM :]
    n_copies = [
        remote(back_out.at[0], back_in.at[0], ns.at[0], nr.at[0], (left, chan)),
        remote(back_out.at[1], back_in.at[1], ns.at[1], nr.at[1], (right, chan)),
    ]
    for copy in n_copies:
        copy.start()
    for copy in h_rims:
        copy.wait_recv()
    h_sides = gather_copies(hrim, hall, rims, hs, hr, NCHAN - 1)
    for copy in h_sides:
        copy.start()
    hall[mine, rims] = hrim[...]
    for copy in n_copies:
        copy.wait_recv()
    for b in range(NB):
        grad = ghown[:, b * BLK : (b + 1) * BLK]
        if b < HB:
            grad = grad + back_in[1, :, b * BLK : (b + 1) * BLK]
        for u in range(HB):
            grad = grad + back_in[0, :, u * BLK : (u + 1) * BLK] * fac[T_LAST + u * NB + b]
        z = zblk[b]
        gate = 1.0 / (1.0 + jnp.exp(-z))
        grad_z = grad * gate * (1.0 + z * (1.0 - gate))
        gblk[b] = grad_z.astype(BF16).astype(F32)
    scan(gblk, T_SLOTS)
    fill_slots(a_z)

    def kernel_grad(whole, a, gsend, grecv, ssem, rsem):
        for n in range(4):
            prod = nt(whole[...], a[n * 256 : (n + 1) * 256, :])
            rows, lanes = (n // 2) * CH, slice((n % 2) * 256, (n % 2) * 256 + 256)
            zall[:, rows : rows + CH, lanes] = prod.reshape(NSPACE, CH, 256)
        gsend[...] = zall[...].astype(BF16)

        @pl.loop(1, NSPACE)
        def _(j):
            to = lax.rem(space + j, NSPACE)
            remote(gsend.at[to], grecv.at[j - 1], ssem.at[j - 1], rsem.at[j - 1], (to, chan)).start()

    def collect(gsend, grecv, ssem, rsem, dst):
        def step(j, total):
            to = lax.rem(space + j, NSPACE)
            remote(gsend.at[to], grecv.at[j - 1], ssem.at[j - 1], rsem.at[j - 1], (to, chan)).wait()
            return total + grecv[j - 1].astype(F32)

        total = lax.fori_loop(1, NSPACE, step, gsend[space].astype(F32))
        dst[: KP // 2, :] = jnp.transpose(total[:CH, :])
        dst[KP // 2 :, :] = jnp.transpose(total[CH:, :])[: KD - KP // 2, :]

    kernel_grad(xall, a_z, gsend1, grecv1, s1s, s1r)

    for copy in h_bodies + h_sides:
        copy.wait_recv()
    kernel_grad(hall, a_g, gsend2, grecv2, s2s, s2r)
    products(w2_ref, hall)
    scan(y, T_ROWS)
    for b in range(NB):
        z = run_end(T_TEND + b)
        out_ref[b * BLK : (b + 1) * BLK, :] = jnp.transpose(z).astype(BF16)

    collect(gsend1, grecv1, s1s, s1r, g1_ref)
    collect(gsend2, grecv2, s2s, s2r, g2_ref)
    for copy in x_rims + x_bodies + x_sides + p_copies + h_rims + h_bodies + h_sides + n_copies:
        copy.wait_send()


def local(features, kernel_map, block_count, weight_one, weight_two, cotangent):
    index, factor = tables(kernel_map, block_count)
    vmem = pl.BlockSpec(memory_space=pltpu.VMEM)
    dma = pltpu.SemaphoreType.DMA
    output, one, two = pl.pallas_call(
        kernel,
        out_shape=(
            jax.ShapeDtypeStruct((OWN, D), BF16),
            jax.ShapeDtypeStruct((KD, CH), F32),
            jax.ShapeDtypeStruct((KD, CH), F32),
        ),
        in_specs=[pl.BlockSpec(memory_space=pltpu.SMEM)] * 2 + [vmem] * 4,
        out_specs=(vmem,) * 3,
        scratch_shapes=[
            pltpu.VMEM((D, OWN), BF16),
            pltpu.VMEM((D, OWN), BF16),
            pltpu.VMEM((D, 2 * RIM), BF16),
            pltpu.VMEM((D, 2 * RIM), BF16),
            pltpu.VMEM((C, EXT), BF16),
            pltpu.VMEM((C, EXT), BF16),
            pltpu.VMEM((C, KP), BF16),
            pltpu.VMEM((NB, D, BLK), F32),
            pltpu.VMEM((NB, D, BLK), F32),
            pltpu.VMEM((NSPACE, 2 * CH, KP // 2), F32),
            pltpu.VMEM((NSLOT, D, BLK), F32),
            pltpu.VMEM((NE, D, BLK), F32),
            pltpu.VMEM((KP, EXT), BF16),
            pltpu.VMEM((KP, EXT), BF16),
            pltpu.VMEM((C, EXT), BF16),
            pltpu.VMEM((NCHAN - 1, D, EXT), BF16),
            pltpu.VMEM((D, EXT), F32),
            pltpu.VMEM((D, RIM), BF16),
            pltpu.VMEM((D, RIM), BF16),
            pltpu.VMEM((2, D, RIM), F32),
            pltpu.VMEM((2, D, RIM), F32),
            pltpu.VMEM((NSPACE, 2 * CH, KP // 2), BF16),
            pltpu.VMEM((NSPACE, 2 * CH, KP // 2), BF16),
            pltpu.VMEM((NSPACE - 1, 2 * CH, KP // 2), BF16),
            pltpu.VMEM((NSPACE - 1, 2 * CH, KP // 2), BF16),
            dma((2 * NCHAN - 2,)),
            dma((2 * NCHAN - 2,)),
            dma((2,)),
            dma((2,)),
            dma((2 * NCHAN - 2,)),
            dma((2 * NCHAN - 2,)),
            dma((2,)),
            dma((2,)),
            dma((NCHAN - 1,)),
            dma((NCHAN - 1,)),
            dma((2,)),
            dma((2,)),
            dma((NSPACE - 1,)),
            dma((NSPACE - 1,)),
            dma((NSPACE - 1,)),
            dma((NSPACE - 1,)),
        ],
        compiler_params=pltpu.CompilerParams(
            collective_id=0, has_side_effects=True, vmem_limit_bytes=56 * 2**20
        ),
    )(index, factor, features, cotangent, weight_one.reshape(KD, C), weight_two.reshape(KD, C))
    return output, one.reshape(K, D, CH), two.reshape(K, D, CH)


def solution(mesh):
    return jax.shard_map(
        local,
        mesh=mesh,
        in_specs=(
            P("space", "chan"),
            P("space", None, None, None),
            P(),
            P(None, "chan", None),
            P(None, "chan", None),
            P("space", "chan"),
        ),
        out_specs=(P("space", "chan"), P(None, "chan", "space"), P(None, "chan", "space")),
        check_vma=False,
    )
```

```python
import jax
import jax.numpy as jnp
from jax import lax
from jax.experimental import pallas as pl
from jax.experimental.pallas import tpu as pltpu
from jax.sharding import PartitionSpec as P

MESH = pl.DeviceIdType.MESH
C = 256
K = 27
BLK = 128
HB = 2
NB = 16
EPK = 16
NX = NB + 2 * HB
NE = K * EPK
NCHAN = 8
NSPACE = 32
D = C // NCHAN
CH = C // NSPACE
KD = K * D
KP = 896
KW = 512
NY = 4
NZ = NSPACE // NY
CY = C // NY
OWN = NB * BLK
RIM = HB * BLK
EXT = NX * BLK
NSLOT = K * NX
F32 = jnp.float32
BF16 = jnp.bfloat16

T_ROWS = 0
T_SLOTS = NE
T_TEND = 2 * NE
T_SEND = T_TEND + NB
T_LAST = T_SEND + NSLOT


def nt(a, b):
    return lax.dot_general(a, b, (((1,), (1,)), ((), ())), preferred_element_type=F32)


def eye(n):
    row = lax.broadcasted_iota(jnp.int32, (n, n), 0)
    col = lax.broadcasted_iota(jnp.int32, (n, n), 1)
    return jnp.where(row == col, 1.0, 0.0).astype(BF16)


def by_core():
    row = lax.broadcasted_iota(jnp.int32, (C, C), 0)
    col = lax.broadcasted_iota(jnp.int32, (C, C), 1)
    core, rest = row // (C // 2), row % (C // 2)
    return jnp.where(col == (rest // D) * (2 * D) + core * D + rest % D, 1.0, 0.0).astype(BF16)


def tables(kernel_map, block_count):
    shard = lax.axis_index("space")
    own = block_count[shard]
    left = block_count[jnp.maximum(shard - 1, 0)]
    entries = kernel_map[0].reshape(NE, 3)
    source, inblock, target = entries[:, 0], entries[:, 1], entries[:, 2]
    pos = jnp.where(
        source == shard,
        inblock,
        jnp.where(source < shard, NB + inblock - (left - HB), NB + HB + inblock),
    )
    live = target < own
    number = jnp.arange(NE, dtype=jnp.int32)
    offset = number // EPK

    def by(key, payload, bits, ends):
        full = key * 512 + number
        rank = jnp.sum((full[None, :] < full[:, None]).astype(jnp.int32), 1)
        value = key * bits + payload
        order = jnp.sum(jnp.where(rank[None, :] == number[:, None], value[None, :], 0), 1)
        keys = order // bits
        same = jnp.concatenate([jnp.zeros((1,), jnp.int32), (keys[1:] == keys[:-1]).astype(jnp.int32)])
        at = jnp.arange(ends, dtype=jnp.int32)[:, None]
        upto = jnp.sum((key[None, :] <= at).astype(jnp.int32), 1)
        there = jnp.sum((key[None, :] == at).astype(jnp.int32), 1)
        return (order % bits, same), (jnp.maximum(upto - 1, 0), (there > 0).astype(jnp.int32))

    rows, tend = by(jnp.where(live, target, NB), pos * K + offset, 1024, NB)
    slots, send = by(jnp.where(live, offset * NX + pos, NSLOT), target, 32, NSLOT)
    last = own - HB + jnp.arange(HB, dtype=jnp.int32)
    which = (last[:, None] == jnp.arange(NB, dtype=jnp.int32)).astype(jnp.int32).reshape(-1)
    index = jnp.concatenate([rows[0], slots[0], tend[0], send[0], last])
    factor = jnp.concatenate([rows[1], slots[1], tend[1], send[1], which])
    return index, factor.astype(F32)


def kernel(
    tab, fac, x_ref, g_ref, w1_ref, w2_ref,
    out_ref, g1_ref, g2_ref,
    xall, hall, xlast, xrim, hlast, hrim, w2t, blocks, zblk, y, run, a_g, a_z,
    part, sibp, comb, via, came, ghown, back_out, back_in,
    ysend1, ysend2, yrecv1, yrecv2, wide, zsend1, zsend2, zrecv1, zrecv2,
    xs, xr, rs, rr, hs, hr, qs, qr, bs, br, cs, cr, ns, nr,
    y1s, y1r, y2s, y2r, z1s, z1r, z2s, z2r,
):
    chan = lax.axis_index("chan")
    space = lax.axis_index("space")
    core = lax.rem(chan, 2)
    chip = chan // 2
    sib = chan + 1 - 2 * core
    ahead = lax.rem(chan + 2, NCHAN)
    behind = lax.rem(chan + NCHAN - 2, NCHAN)
    opposite = lax.rem(chan + NCHAN // 2, NCHAN)
    right = lax.rem(space + 1, NSPACE)
    left = lax.rem(space + NSPACE - 1, NSPACE)
    row = space // NZ
    col = lax.rem(space, NZ)

    def along_y(j):
        return lax.rem(space + j * NZ, NSPACE)

    def along_z(j):
        return row * NZ + lax.rem(col + j, NZ)

    peers = [(space, sib), (space, ahead), (space, behind), (right, chan), (left, chan)]
    peers += [(along_y(j), chan) for j in range(1, NY)] + [(along_z(j), chan) for j in range(1, NZ)]
    barrier = pltpu.get_barrier_semaphore()
    for peer in peers:
        pl.semaphore_signal(barrier, inc=1, device_id=peer, device_id_type=MESH)

    def remote(src, dst, ssem, rsem, device):
        return pltpu.make_async_remote_copy(
            src_ref=src, dst_ref=dst, send_sem=ssem, recv_sem=rsem, device_id=device, device_id_type=MESH
        )

    def channels(who):
        return pl.ds(pl.multiple_of(who * D, D), D)

    mine = channels(chan)
    body = pl.ds(0, OWN)
    rims = pl.ds(OWN, 2 * RIM)
    pending = []

    def start(copy):
        copy.start()
        pending.append(copy)

    class Gather:
        def __init__(self, whole, ssem, rsem):
            half = OWN // 2
            lanes = [pl.ds(0, half), pl.ds(half, half), pl.ds(OWN, RIM), pl.ds(OWN + RIM, RIM)]
            ways = [(chan, ahead), (chan, behind), (chan, sib), None, (behind, sib), (ahead, sib), (opposite, sib)]
            self.copy = {}
            for kind, way in enumerate(ways):
                for p in range(4):
                    origin, to = way or ((behind, ahead), (ahead, behind))[p % 2]
                    ref = whole.at[channels(origin), lanes[p]]
                    n = kind * 4 + p
                    self.copy[kind, p] = remote(ref, ref, ssem.at[n], rsem.at[n], (space, to))

        def send(self, parts):
            for kind in range(3):
                for p in parts:
                    start(self.copy[kind, p])

        def relay(self, parts):
            for p in parts:
                for kind in (0, 1):
                    self.copy[kind, p].wait_recv()
                    if p % 2 == kind:
                        start(self.copy[3, p])
                    start(self.copy[4 + kind, p])

        def finish(self, parts):
            for p in parts:
                self.copy[3, p].wait_recv()
                start(self.copy[6, p])
            for p in parts:
                for kind in (2, 4, 5, 6):
                    self.copy[kind, p].wait_recv()

    def rim_copies(whole, last, rim, ssem, rsem):
        return [
            remote(last, rim.at[:, pl.ds(0, RIM)], ssem.at[0], rsem.at[0], (right, chan)),
            remote(whole.at[mine, pl.ds(0, RIM)], rim.at[:, pl.ds(RIM, RIM)], ssem.at[1], rsem.at[1], (left, chan)),
        ]

    def load_last(last):
        for u in range(HB):
            last[:, u * BLK : (u + 1) * BLK] = blocks[tab[T_LAST + u]].astype(BF16)

    ident = eye(D)
    for b in range(0, NB, 4):
        four = nt(ident, x_ref[b * BLK : (b + 4) * BLK, :])
        xall[mine, b * BLK : (b + 4) * BLK] = four.astype(BF16)
        for u in range(4):
            blocks[b + u] = four[:, u * BLK : (u + 1) * BLK]
    load_last(xlast)

    pl.semaphore_wait(barrier, len(peers))

    x_rims = rim_copies(xall, xlast, xrim, rs, rr)
    for copy in x_rims:
        start(copy)
    x_all = Gather(xall, xs, xr)
    x_all.send((0, 1))

    def scan(src, base):
        def step(i, total):
            for u in range(8):
                n = i * 8 + u
                total = total * fac[base + n] + src[tab[base + n]]
                run[n] = total
            return total

        lax.fori_loop(0, NE // 8, step, jnp.zeros((D, BLK), F32))

    def run_end(at):
        return run[tab[at]] * fac[at]

    def fill_slots(dst):
        @pl.loop(0, K)
        def _(k):
            at = pl.ds(pl.multiple_of(k * D, D), D)
            for p in range(NX):
                dst[at, p * BLK : (p + 1) * BLK] = run_end(T_SEND + k * NX + p).astype(BF16)

    for b in range(0, NB, 4):
        four = nt(ident, g_ref[b * BLK : (b + 4) * BLK, :])
        for u in range(4):
            blocks[b + u] = four[:, u * BLK : (u + 1) * BLK]
    a_g[KD:, :] = jnp.zeros((KP - KD, EXT), BF16)
    a_z[KD:, :] = jnp.zeros((KP - KD, EXT), BF16)
    w2t[:, KD:] = jnp.zeros((C, KP - KD), BF16)
    for copy in x_rims:
        copy.wait_recv()
    xall[mine, rims] = xrim[...]
    x_all.send((2, 3))
    w2t[:, :KD] = nt(by_core(), w2_ref[...]).astype(BF16)
    scan(blocks, T_SLOTS)
    x_all.relay((0, 1))
    fill_slots(a_g)
    x_all.relay((2, 3))

    theirs = pl.ds(pl.multiple_of((1 - core) * (C // 2), C // 2), C // 2)
    ours = pl.ds(pl.multiple_of(core * (C // 2), C // 2), C // 2)
    halves = [pl.ds(0, EXT // 2), pl.ds(EXT // 2, EXT // 2)]
    to_sib = [remote(part.at[theirs, h], sibp.at[:, h], bs.at[i], br.at[i], (space, sib)) for i, h in enumerate(halves)]
    for i in range(2):

        @pl.loop(i * NX // 4, (i + 1) * NX // 4)
        def _(p):
            two = pl.ds(pl.multiple_of(p * 2 * BLK, 2 * BLK), 2 * BLK)
            part[:, two] = jnp.dot(w2t[...], a_g[:, two], preferred_element_type=F32).astype(BF16)

        start(to_sib[i])

    def products(w_ref, whole):
        @pl.loop(0, NX // 2)
        def _(p):
            two = pl.ds(pl.multiple_of(p * 2 * BLK, 2 * BLK), 2 * BLK)
            prod = jnp.dot(w_ref[...], whole[:, two], preferred_element_type=F32)
            y[pl.ds(p * 2 * K, K)] = prod[:, :BLK].reshape(K, D, BLK)
            y[pl.ds(p * 2 * K + K, K)] = prod[:, BLK:].reshape(K, D, BLK)

    x_all.finish((0, 1, 2, 3))
    products(w1_ref, xall)

    def rows_for(chips):
        return pl.ds(pl.multiple_of(lax.rem(chip + chips, NCHAN // 2) * D, D), D)

    to_ahead = [
        remote(comb.at[rows_for(2), halves[0]], via.at[0], cs.at[0], cr.at[0], (space, ahead)),
        remote(comb.at[rows_for(1), halves[1]], came.at[0, :, halves[1]], cs.at[1], cr.at[1], (space, ahead)),
        remote(comb.at[rows_for(1), halves[0]], came.at[0, :, halves[0]], cs.at[2], cr.at[2], (space, ahead)),
    ]
    to_behind = [
        remote(comb.at[rows_for(2), halves[1]], via.at[1], cs.at[3], cr.at[3], (space, behind)),
        remote(comb.at[rows_for(3), halves[0]], came.at[1, :, halves[0]], cs.at[4], cr.at[4], (space, behind)),
        remote(comb.at[rows_for(3), halves[1]], came.at[1, :, halves[1]], cs.at[5], cr.at[5], (space, behind)),
    ]
    for i, h in enumerate(halves):
        to_sib[i].wait_recv()
        comb[:, h] = (part[ours, h].astype(F32) + sibp[:, h].astype(F32)).astype(BF16)
    for i in range(2):
        start(to_ahead[i])
        start(to_behind[i])

    scan(y, T_ROWS)
    to_ahead[0].wait_recv()
    comb[rows_for(1), halves[0]] = (comb[rows_for(1), halves[0]].astype(F32) + via[0].astype(F32)).astype(BF16)
    start(to_ahead[2])
    to_behind[0].wait_recv()
    comb[rows_for(3), halves[1]] = (comb[rows_for(3), halves[1]].astype(F32) + via[1].astype(F32)).astype(BF16)
    start(to_behind[2])

    for b in range(NB):
        z = run_end(T_TEND + b)
        zblk[b] = z
        h = z / (1.0 + jnp.exp(-z))
        blocks[b] = h
        hall[mine, b * BLK : (b + 1) * BLK] = h.astype(BF16)
    load_last(hlast)
    h_rims = rim_copies(hall, hlast, hrim, qs, qr)
    for copy in h_rims:
        start(copy)
    h_all = Gather(hall, hs, hr)
    h_all.send((0, 1))

    for copy in to_ahead[1:] + to_behind[1:]:
        copy.wait_recv()
    for p in range(0, NX, 4):
        at = pl.ds(p * BLK, 4 * BLK)
        ghown[:, at] = comb[rows_for(0), at].astype(F32) + came[0, :, at].astype(F32) + came[1, :, at].astype(F32)
    back_out[0] = ghown[:, OWN : OWN + RIM]
    back_out[1] = ghown[:, OWN + RIM :]
    n_copies = [
        remote(back_out.at[0], back_in.at[0], ns.at[0], nr.at[0], (left, chan)),
        remote(back_out.at[1], back_in.at[1], ns.at[1], nr.at[1], (right, chan)),
    ]
    for copy in n_copies:
        start(copy)
    for copy in h_rims:
        copy.wait_recv()
    hall[mine, rims] = hrim[...]
    h_all.send((2, 3))
    for copy in n_copies:
        copy.wait_recv()
    for b in range(NB):
        grad = ghown[:, b * BLK : (b + 1) * BLK]
        if b < HB:
            grad = grad + back_in[1, :, b * BLK : (b + 1) * BLK]
        for u in range(HB):
            grad = grad + back_in[0, :, u * BLK : (u + 1) * BLK] * fac[T_LAST + u * NB + b]
        z = zblk[b]
        gate = 1.0 / (1.0 + jnp.exp(-z))
        grad_z = grad * gate * (1.0 + z * (1.0 - gate))
        blocks[b] = grad_z.astype(BF16).astype(F32)
    h_all.relay((0, 1))
    scan(blocks, T_SLOTS)
    h_all.relay((2, 3))
    fill_slots(a_z)

    class Sum:
        def __init__(self, ysend, yrecv, zsend, zrecv, ys, yr, zs, zr):
            self.ysend, self.yrecv, self.zsend, self.zrecv = ysend, yrecv, zsend, zrecv
            self.over_y, self.over_z = [], []
            for j in range(1, NY):
                at = pl.ds(pl.multiple_of(lax.rem(row + j, NY) * CY, CY), CY)
                self.over_y.append(
                    remote(ysend.at[at], yrecv.at[j - 1], ys.at[j - 1], yr.at[j - 1], (along_y(j), chan))
                )
            for j in range(1, NZ):
                to = lax.rem(col + j, NZ)
                self.over_z.append(
                    remote(zsend.at[to], zrecv.at[j - 1], zs.at[j - 1], zr.at[j - 1], (along_z(j), chan))
                )

        def begin(self, whole, a):
            for n in range(0, KP, 256):
                at = slice(n, min(n + 256, KP))
                self.ysend[:, at] = nt(whole[...], a[at, :]).astype(BF16)
            for copy in self.over_y:
                start(copy)

        def middle(self):
            for copy in self.over_y:
                copy.wait_recv()
            own = self.ysend[pl.ds(pl.multiple_of(row * CY, CY), CY), :].astype(F32)
            for j in range(NY - 1):
                own = own + self.yrecv[j].astype(F32)
            wide[:, :CH, :] = own[:, :KW].reshape(NZ, CH, KW)
            wide[:, CH:, : KP - KW] = own[:, KW:].reshape(NZ, CH, KP - KW)
            wide[:, CH:, KP - KW :] = jnp.zeros((NZ, CH, 2 * KW - KP), F32)
            self.zsend[...] = wide[...].astype(BF16)
            for copy in self.over_z:
                start(copy)

        def end(self, dst):
            total = self.zsend[col].astype(F32)
            for j, copy in enumerate(self.over_z):
                copy.wait_recv()
                total = total + self.zrecv[j].astype(F32)
            dst[:KW, :] = jnp.transpose(total[:CH, :])
            dst[KW:, :] = jnp.transpose(total[CH:, :])[: KD - KW, :]

    one = Sum(ysend1, yrecv1, zsend1, zrecv1, y1s, y1r, z1s, z1r)
    two = Sum(ysend2, yrecv2, zsend2, zrecv2, y2s, y2r, z2s, z2r)
    one.begin(xall, a_z)

    h_all.finish((0, 1, 2, 3))
    two.begin(hall, a_g)
    one.middle()
    products(w2_ref, hall)
    two.middle()
    scan(y, T_ROWS)
    for b in range(NB):
        z = run_end(T_TEND + b)
        out_ref[b * BLK : (b + 1) * BLK, :] = jnp.transpose(z).astype(BF16)
    one.end(g1_ref)
    two.end(g2_ref)
    for copy in pending:
        copy.wait_send()


def local(features, kernel_map, block_count, weight_one, weight_two, cotangent):
    index, factor = tables(kernel_map, block_count)
    vmem = pl.BlockSpec(memory_space=pltpu.VMEM)

    def v(shape, kind=BF16):
        return pltpu.VMEM(shape, kind)

    def dma(n):
        return [pltpu.SemaphoreType.DMA((n,))] * 2

    output, one, two = pl.pallas_call(
        kernel,
        out_shape=(
            jax.ShapeDtypeStruct((OWN, D), BF16),
            jax.ShapeDtypeStruct((KD, CH), F32),
            jax.ShapeDtypeStruct((KD, CH), F32),
        ),
        in_specs=[pl.BlockSpec(memory_space=pltpu.SMEM)] * 2 + [vmem] * 4,
        out_specs=(vmem,) * 3,
        scratch_shapes=[
            v((C, EXT)), v((C, EXT)), v((D, RIM)), v((D, 2 * RIM)), v((D, RIM)), v((D, 2 * RIM)),
            v((C, KP)), v((NB, D, BLK), F32), v((NB, D, BLK), F32), v((NSLOT, D, BLK), F32), v((NE, D, BLK), F32),
            v((KP, EXT)), v((KP, EXT)),
            v((C, EXT)), v((C // 2, EXT)), v((C // 2, EXT)), v((2, D, EXT // 2)), v((2, D, EXT)),
            v((D, EXT), F32), v((2, D, RIM), F32), v((2, D, RIM), F32),
            v((C, KP)), v((C, KP)), v((NY - 1, CY, KP)), v((NY - 1, CY, KP)),
            v((NZ, 2 * CH, KW), F32), v((NZ, 2 * CH, KW)), v((NZ, 2 * CH, KW)),
            v((NZ - 1, 2 * CH, KW)), v((NZ - 1, 2 * CH, KW)),
            *dma(28), *dma(2), *dma(28), *dma(2), *dma(2), *dma(6), *dma(2),
            *dma(NY - 1), *dma(NY - 1), *dma(NZ - 1), *dma(NZ - 1),
        ],
        compiler_params=pltpu.CompilerParams(
            collective_id=0, has_side_effects=True, vmem_limit_bytes=56 * 2**20
        ),
    )(index, factor, features, cotangent, weight_one.reshape(KD, C), weight_two.reshape(KD, C))
    return output, one.reshape(K, D, CH), two.reshape(K, D, CH)


def solution(mesh):
    return jax.shard_map(
        local,
        mesh=mesh,
        in_specs=(
            P("space", "chan"),
            P("space", None, None, None),
            P(),
            P(None, "chan", None),
            P(None, "chan", None),
            P("space", "chan"),
        ),
        out_specs=(P("space", "chan"), P(None, "chan", "space"), P(None, "chan", "space")),
        check_vma=False,
    )
```

```python
import jax
import jax.numpy as jnp
from jax import lax
from jax.experimental import pallas as pl
from jax.experimental.pallas import tpu as pltpu
from jax.sharding import PartitionSpec as P

MESH = pl.DeviceIdType.MESH
C = 256
K = 27
BLK = 128
HB = 2
NB = 16
EPK = 16
NX = NB + 2 * HB
NE = K * EPK
NCHAN = 8
NSPACE = 32
D = C // NCHAN
CH = C // NSPACE
KD = K * D
KP = 896
KW = 512
NY = 4
NZ = NSPACE // NY
CY = C // NY
OWN = NB * BLK
RIM = HB * BLK
EXT = NX * BLK
NSLOT = K * NX
F32 = jnp.float32
BF16 = jnp.bfloat16

NP = 512
TW = 640
T_ROWS, T_SLOTS, T_TEND, T_SEND, T_LAST = 0, 1, 2, 3, 4


def nt(a, b):
    return lax.dot_general(a, b, (((1,), (1,)), ((), ())), preferred_element_type=F32)


def by_core():
    row = lax.broadcasted_iota(jnp.int32, (C, C), 0)
    col = lax.broadcasted_iota(jnp.int32, (C, C), 1)
    core, rest = row // (C // 2), row % (C // 2)
    return jnp.where(col == (rest // D) * (2 * D) + core * D + rest % D, 1.0, 0.0).astype(BF16)


def iota(shape, dim):
    return lax.broadcasted_iota(jnp.int32, shape, dim)


def total(cond, axis):
    return jnp.sum(jnp.where(cond, 1.0, 0.0), axis, keepdims=True)


def tables(count_ref, km_ref, index, factor):
    shard = lax.axis_index("space")
    own, left = count_ref[shard], count_ref[jnp.maximum(shard - 1, 0)]
    index[...] = jnp.zeros(index.shape, jnp.int32)
    factor[...] = jnp.zeros(factor.shape, F32)
    shard, own, left = shard.astype(F32), own.astype(F32), left.astype(F32)
    spread = jnp.where((iota((K, NP), 1) & 31) == iota((K, NP), 0), 1.0, 0.0).astype(BF16)
    gather = jnp.where((iota((NP, K), 0) & 31) == iota((NP, K), 1), 1.0, 0.0).astype(BF16)
    at_row = (iota((EPK, NP), 1) >> 5) == iota((EPK, NP), 0)
    at_col = (iota((NP, EPK), 0) >> 5) == iota((NP, EPK), 1)

    def keys(form, axis):
        shape = (1, NP) if axis == 0 else (NP, 1)
        number = iota(shape, 1 - axis)
        offset = number & 31
        source, inblock, target = (form(km_ref[c].astype(BF16)) for c in range(3))
        before = NB + inblock - (left - HB)
        pos = jnp.where(source == shard, inblock, jnp.where(source < shard, before, NB + HB + inblock))
        pos = jnp.clip(pos, 0.0, NX - 1.0)
        target = jnp.clip(target, 0.0, NB - 1.0)
        gone = jnp.maximum(jnp.where(target < own, 0.0, 1.0), jnp.where(offset < K, 0.0, 1.0)) > 0.5
        known = offset < K
        offset = offset.astype(F32)
        by_target = jnp.where(gone, 1.0 * NB, target)
        by_slot = jnp.where(gone, 1.0 * NSLOT, offset * NX + pos)
        product = jnp.where(known, pos * K + offset, 0.0)
        return number.astype(F32), (by_target, by_slot), (product, target)

    def as_row(v):
        wide = jnp.dot(v, spread, preferred_element_type=F32)
        return jnp.sum(jnp.where(at_row, wide, 0.0), 0, keepdims=True)

    def as_col(v):
        return jnp.sum(jnp.where(at_col, nt(gather, v), 0.0), 1, keepdims=True)

    n_row, key_row, _ = keys(as_row, 0)
    n_col, key_col, pay_col = keys(as_col, 1)
    for i, width in enumerate((BLK, TW)):
        key = key_col[i]
        rank = total(key_row[i] * NP + n_row < key * NP + n_col, 1)
        sorted_key = jnp.sum(jnp.where(rank == n_row, key, 0.0), 0, keepdims=True)
        index[i : i + 1, :NP] = jnp.sum(jnp.where(rank == n_row, pay_col[i], 0.0), 0, keepdims=True).astype(jnp.int32)
        factor[i : i + 1, :NP] = jnp.where(total(key < sorted_key, 0) == n_row, 0.0, 1.0)
        at = iota((1, width), 1).astype(F32)
        upto = total(key <= at, 0)
        index[T_TEND + i : T_TEND + i + 1, :width] = jnp.clip(upto - 1.0, 0.0, NE - 1.0).astype(jnp.int32)
        factor[T_TEND + i : T_TEND + i + 1, :width] = jnp.minimum(total(key == at, 0), 1.0)
    block = iota((1, BLK), 1).astype(F32)
    last = jnp.clip(own - HB + block, 0.0, NB - 1.0)
    index[T_LAST : T_LAST + 1, :BLK] = last.astype(jnp.int32)
    for u in range(HB):
        factor[T_LAST + u : T_LAST + u + 1, :BLK] = jnp.where(block == own - HB + u, 1.0, 0.0)


def kernel(
    tab, fac, x_ref, g_ref, w1_ref, w2_ref,
    out_ref, g1_ref, g2_ref,
    xall, hall, xlast, xrim, hlast, hrim, w2t, blocks, zblk, y, run, a_g, a_z,
    part, sibp, comb, via, came, ghown, back_out, back_in,
    ysend1, ysend2, yrecv1, yrecv2, wide, zsend1, zsend2, zrecv1, zrecv2,
    xs, xr, rs, rr, hs, hr, qs, qr, bs, br, cs, cr, ns, nr,
    y1s, y1r, y2s, y2r, z1s, z1r, z2s, z2r,
):
    chan = lax.axis_index("chan")
    space = lax.axis_index("space")
    core = lax.rem(chan, 2)
    chip = chan // 2
    sib = chan + 1 - 2 * core
    ahead = lax.rem(chan + 2, NCHAN)
    behind = lax.rem(chan + NCHAN - 2, NCHAN)
    opposite = lax.rem(chan + NCHAN // 2, NCHAN)
    right = lax.rem(space + 1, NSPACE)
    left = lax.rem(space + NSPACE - 1, NSPACE)
    row = space // NZ
    col = lax.rem(space, NZ)

    def along_y(j):
        return lax.rem(space + j * NZ, NSPACE)

    def along_z(j):
        return row * NZ + lax.rem(col + j, NZ)

    peers = [(space, sib), (space, ahead), (space, behind), (right, chan), (left, chan)]
    peers += [(along_y(j), chan) for j in range(1, NY)] + [(along_z(j), chan) for j in range(1, NZ)]
    barrier = pltpu.get_barrier_semaphore()
    for peer in peers:
        pl.semaphore_signal(barrier, inc=1, device_id=peer, device_id_type=MESH)

    def remote(src, dst, ssem, rsem, device):
        return pltpu.make_async_remote_copy(
            src_ref=src, dst_ref=dst, send_sem=ssem, recv_sem=rsem, device_id=device, device_id_type=MESH
        )

    def channels(who):
        return pl.ds(pl.multiple_of(who * D, D), D)

    mine = channels(chan)
    body = pl.ds(0, OWN)
    rims = pl.ds(OWN, 2 * RIM)
    pending = []

    def start(copy):
        copy.start()
        pending.append(copy)

    class Gather:
        def __init__(self, whole, ssem, rsem):
            half = OWN // 2
            lanes = [pl.ds(0, half), pl.ds(half, half), pl.ds(OWN, RIM), pl.ds(OWN + RIM, RIM)]
            ways = [(chan, ahead), (chan, behind), (chan, sib), None, (behind, sib), (ahead, sib), (opposite, sib)]
            self.copy = {}
            for kind, way in enumerate(ways):
                for p in range(4):
                    origin, to = way or ((behind, ahead), (ahead, behind))[p % 2]
                    ref = whole.at[channels(origin), lanes[p]]
                    n = kind * 4 + p
                    self.copy[kind, p] = remote(ref, ref, ssem.at[n], rsem.at[n], (space, to))

        def send(self, parts):
            for kind in range(3):
                for p in parts:
                    start(self.copy[kind, p])

        def relay(self, parts):
            for p in parts:
                for kind in (0, 1):
                    self.copy[kind, p].wait_recv()
                    if p % 2 == kind:
                        start(self.copy[3, p])
                    start(self.copy[4 + kind, p])

        def finish(self, parts):
            for p in parts:
                self.copy[3, p].wait_recv()
                start(self.copy[6, p])
            for p in parts:
                for kind in (2, 4, 5, 6):
                    self.copy[kind, p].wait_recv()

    def rim_copies(whole, last, rim, ssem, rsem):
        return [
            remote(last, rim.at[:, pl.ds(0, RIM)], ssem.at[0], rsem.at[0], (right, chan)),
            remote(whole.at[mine, pl.ds(0, RIM)], rim.at[:, pl.ds(RIM, RIM)], ssem.at[1], rsem.at[1], (left, chan)),
        ]

    def load_last(last):
        for u in range(HB):
            last[:, u * BLK : (u + 1) * BLK] = blocks[tab[T_LAST, u]].astype(BF16)

    xall[mine, body] = x_ref[...]
    for b in range(NB):
        blocks[b] = x_ref[:, b * BLK : (b + 1) * BLK].astype(F32)
    load_last(xlast)

    pl.semaphore_wait(barrier, len(peers))

    x_rims = rim_copies(xall, xlast, xrim, rs, rr)
    for copy in x_rims:
        start(copy)
    x_all = Gather(xall, xs, xr)
    x_all.send((0, 1))

    def scan(src, base):
        def step(i, total):
            for u in range(8):
                n = i * 8 + u
                total = total * fac[base, n] + src[tab[base, n]]
                run[n] = total
            return total

        lax.fori_loop(0, NE // 8, step, jnp.zeros((D, BLK), F32))

    def run_end(table, at):
        return run[tab[table, at]] * fac[table, at]

    def fill_slots(dst):
        @pl.loop(0, K)
        def _(k):
            at = pl.ds(pl.multiple_of(k * D, D), D)
            for p in range(NX):
                dst[at, p * BLK : (p + 1) * BLK] = run_end(T_SEND, k * NX + p).astype(BF16)

    for b in range(NB):
        blocks[b] = g_ref[:, b * BLK : (b + 1) * BLK].astype(F32)
    a_g[KD:, :] = jnp.zeros((KP - KD, EXT), BF16)
    a_z[KD:, :] = jnp.zeros((KP - KD, EXT), BF16)
    w2t[:, KD:] = jnp.zeros((C, KP - KD), BF16)
    for copy in x_rims:
        copy.wait_recv()
    xall[mine, rims] = xrim[...]
    x_all.send((2, 3))
    w2t[:, :KD] = nt(by_core(), w2_ref[...]).astype(BF16)
    scan(blocks, T_SLOTS)
    x_all.relay((0, 1))
    fill_slots(a_g)
    x_all.relay((2, 3))

    theirs = pl.ds(pl.multiple_of((1 - core) * (C // 2), C // 2), C // 2)
    ours = pl.ds(pl.multiple_of(core * (C // 2), C // 2), C // 2)
    halves = [pl.ds(0, EXT // 2), pl.ds(EXT // 2, EXT // 2)]
    to_sib = [remote(part.at[theirs, h], sibp.at[:, h], bs.at[i], br.at[i], (space, sib)) for i, h in enumerate(halves)]
    for i in range(2):

        @pl.loop(i * NX // 4, (i + 1) * NX // 4)
        def _(p):
            two = pl.ds(pl.multiple_of(p * 2 * BLK, 2 * BLK), 2 * BLK)
            part[:, two] = jnp.dot(w2t[...], a_g[:, two], preferred_element_type=F32).astype(BF16)

        start(to_sib[i])

    def products(w_ref, whole):
        @pl.loop(0, NX // 2)
        def _(p):
            two = pl.ds(pl.multiple_of(p * 2 * BLK, 2 * BLK), 2 * BLK)
            prod = jnp.dot(w_ref[...], whole[:, two], preferred_element_type=F32)
            y[pl.ds(p * 2 * K, K)] = prod[:, :BLK].reshape(K, D, BLK)
            y[pl.ds(p * 2 * K + K, K)] = prod[:, BLK:].reshape(K, D, BLK)

    x_all.finish((0, 1, 2, 3))
    products(w1_ref, xall)

    def rows_for(chips):
        return pl.ds(pl.multiple_of(lax.rem(chip + chips, NCHAN // 2) * D, D), D)

    to_ahead = [
        remote(comb.at[rows_for(2), halves[0]], via.at[0], cs.at[0], cr.at[0], (space, ahead)),
        remote(comb.at[rows_for(1), halves[1]], came.at[0, :, halves[1]], cs.at[1], cr.at[1], (space, ahead)),
        remote(comb.at[rows_for(1), halves[0]], came.at[0, :, halves[0]], cs.at[2], cr.at[2], (space, ahead)),
    ]
    to_behind = [
        remote(comb.at[rows_for(2), halves[1]], via.at[1], cs.at[3], cr.at[3], (space, behind)),
        remote(comb.at[rows_for(3), halves[0]], came.at[1, :, halves[0]], cs.at[4], cr.at[4], (space, behind)),
        remote(comb.at[rows_for(3), halves[1]], came.at[1, :, halves[1]], cs.at[5], cr.at[5], (space, behind)),
    ]
    for i, h in enumerate(halves):
        to_sib[i].wait_recv()
        comb[:, h] = (part[ours, h].astype(F32) + sibp[:, h].astype(F32)).astype(BF16)
    for i in range(2):
        start(to_ahead[i])
        start(to_behind[i])

    scan(y, T_ROWS)
    to_ahead[0].wait_recv()
    comb[rows_for(1), halves[0]] = (comb[rows_for(1), halves[0]].astype(F32) + via[0].astype(F32)).astype(BF16)
    start(to_ahead[2])
    to_behind[0].wait_recv()
    comb[rows_for(3), halves[1]] = (comb[rows_for(3), halves[1]].astype(F32) + via[1].astype(F32)).astype(BF16)
    start(to_behind[2])

    for b in range(NB):
        z = run_end(T_TEND, b)
        zblk[b] = z
        h = z / (1.0 + jnp.exp(-z))
        blocks[b] = h
        hall[mine, b * BLK : (b + 1) * BLK] = h.astype(BF16)
    load_last(hlast)
    h_rims = rim_copies(hall, hlast, hrim, qs, qr)
    for copy in h_rims:
        start(copy)
    h_all = Gather(hall, hs, hr)
    h_all.send((0, 1))

    for copy in to_ahead[1:] + to_behind[1:]:
        copy.wait_recv()
    for p in range(0, NX, 4):
        at = pl.ds(p * BLK, 4 * BLK)
        ghown[:, at] = comb[rows_for(0), at].astype(F32) + came[0, :, at].astype(F32) + came[1, :, at].astype(F32)
    back_out[0] = ghown[:, OWN : OWN + RIM]
    back_out[1] = ghown[:, OWN + RIM :]
    n_copies = [
        remote(back_out.at[0], back_in.at[0], ns.at[0], nr.at[0], (left, chan)),
        remote(back_out.at[1], back_in.at[1], ns.at[1], nr.at[1], (right, chan)),
    ]
    for copy in n_copies:
        start(copy)
    for copy in h_rims:
        copy.wait_recv()
    hall[mine, rims] = hrim[...]
    h_all.send((2, 3))
    for copy in n_copies:
        copy.wait_recv()
    for b in range(NB):
        grad = ghown[:, b * BLK : (b + 1) * BLK]
        if b < HB:
            grad = grad + back_in[1, :, b * BLK : (b + 1) * BLK]
        for u in range(HB):
            grad = grad + back_in[0, :, u * BLK : (u + 1) * BLK] * fac[T_LAST + u, b]
        z = zblk[b]
        gate = 1.0 / (1.0 + jnp.exp(-z))
        grad_z = grad * gate * (1.0 + z * (1.0 - gate))
        blocks[b] = grad_z.astype(BF16).astype(F32)
    h_all.relay((0, 1))
    scan(blocks, T_SLOTS)
    h_all.relay((2, 3))
    fill_slots(a_z)

    class Sum:
        def __init__(self, ysend, yrecv, zsend, zrecv, ys, yr, zs, zr):
            self.ysend, self.yrecv, self.zsend, self.zrecv = ysend, yrecv, zsend, zrecv
            self.over_y, self.over_z = [], []
            for j in range(1, NY):
                at = pl.ds(pl.multiple_of(lax.rem(row + j, NY) * CY, CY), CY)
                self.over_y.append(
                    remote(ysend.at[at], yrecv.at[j - 1], ys.at[j - 1], yr.at[j - 1], (along_y(j), chan))
                )
            for j in range(1, NZ):
                to = lax.rem(col + j, NZ)
                self.over_z.append(
                    remote(zsend.at[to], zrecv.at[j - 1], zs.at[j - 1], zr.at[j - 1], (along_z(j), chan))
                )

        def begin(self, whole, a):
            for n in range(0, KP, 256):
                at = slice(n, min(n + 256, KP))
                self.ysend[:, at] = nt(whole[...], a[at, :]).astype(BF16)
            for copy in self.over_y:
                start(copy)

        def middle(self):
            for copy in self.over_y:
                copy.wait_recv()
            own = self.ysend[pl.ds(pl.multiple_of(row * CY, CY), CY), :].astype(F32)
            for j in range(NY - 1):
                own = own + self.yrecv[j].astype(F32)
            wide[:, :CH, :] = own[:, :KW].reshape(NZ, CH, KW)
            wide[:, CH:, : KP - KW] = own[:, KW:].reshape(NZ, CH, KP - KW)
            wide[:, CH:, KP - KW :] = jnp.zeros((NZ, CH, 2 * KW - KP), F32)
            self.zsend[...] = wide[...].astype(BF16)
            for copy in self.over_z:
                start(copy)

        def end(self, dst):
            total = self.zsend[col].astype(F32)
            for j, copy in enumerate(self.over_z):
                copy.wait_recv()
                total = total + self.zrecv[j].astype(F32)
            for k in range(K):
                rows, at = (k * D // KW) * CH, k * D % KW
                dst[k] = total[rows : rows + CH, at : at + D]

    one = Sum(ysend1, yrecv1, zsend1, zrecv1, y1s, y1r, z1s, z1r)
    two = Sum(ysend2, yrecv2, zsend2, zrecv2, y2s, y2r, z2s, z2r)
    one.begin(xall, a_z)

    h_all.finish((0, 1, 2, 3))
    two.begin(hall, a_g)
    one.middle()
    products(w2_ref, hall)
    two.middle()
    scan(y, T_ROWS)
    for b in range(NB):
        z = run_end(T_TEND, b)
        out_ref[:, b * BLK : (b + 1) * BLK] = z.astype(BF16)
    one.end(g1_ref)
    two.end(g2_ref)
    for copy in pending:
        copy.wait_send()


def local(features, kernel_map, block_count, weight_one, weight_two, cotangent):
    vmem = pl.BlockSpec(memory_space=pltpu.VMEM)
    smem = pl.BlockSpec(memory_space=pltpu.SMEM)
    index, factor = pl.pallas_call(
        tables,
        out_shape=(jax.ShapeDtypeStruct((8, TW), jnp.int32), jax.ShapeDtypeStruct((8, TW), F32)),
        in_specs=[smem, vmem],
        out_specs=(vmem, vmem),
    )(block_count, kernel_map[0].transpose(2, 1, 0))

    def v(shape, kind=BF16):
        return pltpu.VMEM(shape, kind)

    def dma(n):
        return [pltpu.SemaphoreType.DMA((n,))] * 2

    output, one, two = pl.pallas_call(
        kernel,
        out_shape=(
            jax.ShapeDtypeStruct((D, OWN), BF16),
            jax.ShapeDtypeStruct((K, CH, D), F32),
            jax.ShapeDtypeStruct((K, CH, D), F32),
        ),
        in_specs=[smem] * 2 + [vmem] * 4,
        out_specs=(vmem,) * 3,
        scratch_shapes=[
            v((C, EXT)), v((C, EXT)), v((D, RIM)), v((D, 2 * RIM)), v((D, RIM)), v((D, 2 * RIM)),
            v((C, KP)), v((NB, D, BLK), F32), v((NB, D, BLK), F32), v((NSLOT, D, BLK), F32), v((NE, D, BLK), F32),
            v((KP, EXT)), v((KP, EXT)),
            v((C, EXT)), v((C // 2, EXT)), v((C // 2, EXT)), v((2, D, EXT // 2)), v((2, D, EXT)),
            v((D, EXT), F32), v((2, D, RIM), F32), v((2, D, RIM), F32),
            v((C, KP)), v((C, KP)), v((NY - 1, CY, KP)), v((NY - 1, CY, KP)),
            v((NZ, 2 * CH, KW), F32), v((NZ, 2 * CH, KW)), v((NZ, 2 * CH, KW)),
            v((NZ - 1, 2 * CH, KW)), v((NZ - 1, 2 * CH, KW)),
            *dma(28), *dma(2), *dma(28), *dma(2), *dma(2), *dma(6), *dma(2),
            *dma(NY - 1), *dma(NY - 1), *dma(NZ - 1), *dma(NZ - 1),
        ],
        compiler_params=pltpu.CompilerParams(
            collective_id=0, has_side_effects=True, vmem_limit_bytes=56 * 2**20
        ),
    )(
        index,
        factor,
        features.T,
        cotangent.T,
        weight_one.reshape(KD, C),
        weight_two.reshape(KD, C),
    )
    return output.T, one.transpose(0, 2, 1), two.transpose(0, 2, 1)


def solution(mesh):
    return jax.shard_map(
        local,
        mesh=mesh,
        in_specs=(
            P("space", "chan"),
            P("space", None, None, None),
            P(),
            P(None, "chan", None),
            P(None, "chan", None),
            P("space", "chan"),
        ),
        out_specs=(P("space", "chan"), P(None, "chan", "space"), P(None, "chan", "space")),
        check_vma=False,
    )
```

```python
import jax
import jax.numpy as jnp
from jax import lax
from jax.experimental import pallas as pl
from jax.experimental.pallas import tpu as pltpu
from jax.sharding import PartitionSpec as P

MESH = pl.DeviceIdType.MESH
C = 256
K = 27
BLK = 128
HB = 2
NB = 16
EPK = 16
NX = NB + 2 * HB
NE = K * EPK
NCHAN = 8
NSPACE = 32
D = C // NCHAN
CH = C // NSPACE
KD = K * D
KP = 896
KW = 512
NY = 4
NZ = NSPACE // NY
CY = C // NY
OWN = NB * BLK
RIM = HB * BLK
EXT = NX * BLK
NSLOT = K * NX
F32 = jnp.float32
BF16 = jnp.bfloat16

NP = 512
TW = 640
T_ROWS, T_SLOTS, T_TEND, T_SEND, T_LAST = 0, 1, 2, 3, 4


def nt(a, b):
    return lax.dot_general(a, b, (((1,), (1,)), ((), ())), preferred_element_type=F32)


def by_core():
    row = lax.broadcasted_iota(jnp.int32, (C, C), 0)
    col = lax.broadcasted_iota(jnp.int32, (C, C), 1)
    core, rest = row // (C // 2), row % (C // 2)
    return jnp.where(col == (rest // D) * (2 * D) + core * D + rest % D, 1.0, 0.0).astype(BF16)


def iota(shape, dim):
    return lax.broadcasted_iota(jnp.int32, shape, dim)


def total(cond, axis):
    return jnp.sum(jnp.where(cond, 1.0, 0.0), axis, keepdims=True)


def tables(count_ref, km_ref, index, factor):
    shard = lax.axis_index("space")
    own, left = count_ref[shard], count_ref[jnp.maximum(shard - 1, 0)]
    index[...] = jnp.zeros(index.shape, jnp.int32)
    factor[...] = jnp.zeros(factor.shape, F32)
    shard, own, left = shard.astype(F32), own.astype(F32), left.astype(F32)
    spread = jnp.where((iota((K, NP), 1) & 31) == iota((K, NP), 0), 1.0, 0.0).astype(BF16)
    gather = jnp.where((iota((NP, K), 0) & 31) == iota((NP, K), 1), 1.0, 0.0).astype(BF16)
    at_row = (iota((EPK, NP), 1) >> 5) == iota((EPK, NP), 0)
    at_col = (iota((NP, EPK), 0) >> 5) == iota((NP, EPK), 1)

    def keys(form, axis):
        shape = (1, NP) if axis == 0 else (NP, 1)
        number = iota(shape, 1 - axis)
        offset = number & 31
        source, inblock, target = (form(km_ref[c].astype(BF16)) for c in range(3))
        before = NB + inblock - (left - HB)
        pos = jnp.where(source == shard, inblock, jnp.where(source < shard, before, NB + HB + inblock))
        pos = jnp.clip(pos, 0.0, NX - 1.0)
        target = jnp.clip(target, 0.0, NB - 1.0)
        gone = jnp.maximum(jnp.where(target < own, 0.0, 1.0), jnp.where(offset < K, 0.0, 1.0)) > 0.5
        known = offset < K
        offset = offset.astype(F32)
        by_target = jnp.where(gone, 1.0 * NB, target)
        by_slot = jnp.where(gone, 1.0 * NSLOT, offset * NX + pos)
        product = jnp.where(known, pos * K + offset, 0.0)
        return number.astype(F32), (by_target, by_slot), (product, target)

    def as_row(v):
        wide = jnp.dot(v, spread, preferred_element_type=F32)
        return jnp.sum(jnp.where(at_row, wide, 0.0), 0, keepdims=True)

    def as_col(v):
        return jnp.sum(jnp.where(at_col, nt(gather, v), 0.0), 1, keepdims=True)

    n_row, key_row, _ = keys(as_row, 0)
    n_col, key_col, pay_col = keys(as_col, 1)
    for i, width in enumerate((BLK, TW)):
        key = key_col[i]
        rank = total(key_row[i] * NP + n_row < key * NP + n_col, 1)
        sorted_key = jnp.sum(jnp.where(rank == n_row, key, 0.0), 0, keepdims=True)
        index[i : i + 1, :NP] = jnp.sum(jnp.where(rank == n_row, pay_col[i], 0.0), 0, keepdims=True).astype(jnp.int32)
        factor[i : i + 1, :NP] = jnp.where(total(key < sorted_key, 0) == n_row, 0.0, 1.0)
        at = iota((1, width), 1).astype(F32)
        upto = total(key <= at, 0)
        index[T_TEND + i : T_TEND + i + 1, :width] = jnp.clip(upto - 1.0, 0.0, NE - 1.0).astype(jnp.int32)
        factor[T_TEND + i : T_TEND + i + 1, :width] = jnp.minimum(total(key == at, 0), 1.0)
    block = iota((1, BLK), 1).astype(F32)
    last = jnp.clip(own - HB + block, 0.0, NB - 1.0)
    index[T_LAST : T_LAST + 1, :BLK] = last.astype(jnp.int32)
    for u in range(HB):
        factor[T_LAST + u : T_LAST + u + 1, :BLK] = jnp.where(block == own - HB + u, 1.0, 0.0)


def kernel(
    tab, fac, x_ref, g_ref, w1_ref, w2_ref,
    out_ref, g1_ref, g2_ref,
    xall, hall, xlast, xrim, hlast, hrim, w2t, blocks, zblk, y, run, a_g, a_z,
    part, sibp, comb, via, came, ghown, back_out, back_in,
    ysend1, ysend2, yrecv1, yrecv2, wide, zsend1, zsend2, zrecv1, zrecv2,
    xs, xr, rs, rr, hs, hr, qs, qr, bs, br, cs, cr, ns, nr,
    y1s, y1r, y2s, y2r, z1s, z1r, z2s, z2r,
):
    chan = lax.axis_index("chan")
    space = lax.axis_index("space")
    core = lax.rem(chan, 2)
    chip = chan // 2
    sib = chan + 1 - 2 * core
    ahead = lax.rem(chan + 2, NCHAN)
    behind = lax.rem(chan + NCHAN - 2, NCHAN)
    opposite = lax.rem(chan + NCHAN // 2, NCHAN)
    right = lax.rem(space + 1, NSPACE)
    left = lax.rem(space + NSPACE - 1, NSPACE)
    row = space // NZ
    col = lax.rem(space, NZ)

    def along_y(j):
        return lax.rem(space + j * NZ, NSPACE)

    def along_z(j):
        return row * NZ + lax.rem(col + j, NZ)

    peers = [(space, sib), (space, ahead), (space, behind), (right, chan), (left, chan)]
    peers += [(along_y(j), chan) for j in range(1, NY)] + [(along_z(j), chan) for j in range(1, NZ)]
    barrier = pltpu.get_barrier_semaphore()
    for peer in peers:
        pl.semaphore_signal(barrier, inc=1, device_id=peer, device_id_type=MESH)

    def remote(src, dst, ssem, rsem, device):
        return pltpu.make_async_remote_copy(
            src_ref=src, dst_ref=dst, send_sem=ssem, recv_sem=rsem, device_id=device, device_id_type=MESH
        )

    def channels(who):
        return pl.ds(pl.multiple_of(who * D, D), D)

    mine = channels(chan)
    body = pl.ds(0, OWN)
    rims = pl.ds(OWN, 2 * RIM)
    pending = []

    def start(copy):
        copy.start()
        pending.append(copy)

    class Gather:
        def __init__(self, whole, ssem, rsem):
            half = OWN // 2
            lanes = [pl.ds(0, half), pl.ds(half, half), pl.ds(OWN, RIM), pl.ds(OWN + RIM, RIM)]
            ways = [(chan, ahead), (chan, behind), (chan, sib), None, (behind, sib), (ahead, sib), (opposite, sib)]
            self.copy = {}
            for kind, way in enumerate(ways):
                for p in range(4):
                    origin, to = way or ((behind, ahead), (ahead, behind))[p % 2]
                    ref = whole.at[channels(origin), lanes[p]]
                    n = kind * 4 + p
                    self.copy[kind, p] = remote(ref, ref, ssem.at[n], rsem.at[n], (space, to))

        def send(self, parts):
            for kind in range(3):
                for p in parts:
                    start(self.copy[kind, p])

        def relay(self, parts):
            for p in parts:
                for kind in (0, 1):
                    self.copy[kind, p].wait_recv()
                    if p % 2 == kind:
                        start(self.copy[3, p])
                    start(self.copy[4 + kind, p])

        def finish(self, parts):
            for p in parts:
                self.copy[3, p].wait_recv()
                start(self.copy[6, p])
            for p in parts:
                for kind in (2, 4, 5, 6):
                    self.copy[kind, p].wait_recv()

    def rim_copies(whole, last, rim, ssem, rsem):
        return [
            remote(last, rim.at[:, pl.ds(0, RIM)], ssem.at[0], rsem.at[0], (right, chan)),
            remote(whole.at[mine, pl.ds(0, RIM)], rim.at[:, pl.ds(RIM, RIM)], ssem.at[1], rsem.at[1], (left, chan)),
        ]

    def load_last(last):
        for u in range(HB):
            last[:, u * BLK : (u + 1) * BLK] = blocks[tab[T_LAST, u]].astype(BF16)

    xall[mine, body] = x_ref[...]
    for b in range(NB):
        blocks[b] = x_ref[:, b * BLK : (b + 1) * BLK].astype(F32)
    load_last(xlast)

    pl.semaphore_wait(barrier, len(peers))

    x_rims = rim_copies(xall, xlast, xrim, rs, rr)
    for copy in x_rims:
        start(copy)
    x_all = Gather(xall, xs, xr)
    x_all.send((0, 1))

    def scan(src, base):
        def step(i, total):
            for u in range(8):
                n = i * 8 + u
                total = total * fac[base, n] + src[tab[base, n]]
                run[n] = total
            return total

        lax.fori_loop(0, NE // 8, step, jnp.zeros((D, BLK), F32))

    def run_end(table, at):
        return run[tab[table, at]] * fac[table, at]

    def fill_slots(dst):
        @pl.loop(0, K)
        def _(k):
            at = pl.ds(pl.multiple_of(k * D, D), D)
            for p in range(NX):
                dst[at, p * BLK : (p + 1) * BLK] = run_end(T_SEND, k * NX + p).astype(BF16)

    for b in range(NB):
        blocks[b] = g_ref[:, b * BLK : (b + 1) * BLK].astype(F32)
    a_g[KD:, :] = jnp.zeros((KP - KD, EXT), BF16)
    a_z[KD:, :] = jnp.zeros((KP - KD, EXT), BF16)
    w2t[:, KD:] = jnp.zeros((C, KP - KD), BF16)
    for copy in x_rims:
        copy.wait_recv()
    xall[mine, rims] = xrim[...]
    x_all.send((2, 3))
    w2t[:, :KD] = nt(by_core(), w2_ref[...]).astype(BF16)
    scan(blocks, T_SLOTS)
    x_all.relay((0, 1))
    fill_slots(a_g)
    x_all.relay((2, 3))

    theirs = pl.ds(pl.multiple_of((1 - core) * (C // 2), C // 2), C // 2)
    ours = pl.ds(pl.multiple_of(core * (C // 2), C // 2), C // 2)
    halves = [pl.ds(0, EXT // 2), pl.ds(EXT // 2, EXT // 2)]
    to_sib = [remote(part.at[theirs, h], sibp.at[:, h], bs.at[i], br.at[i], (space, sib)) for i, h in enumerate(halves)]
    for i in range(2):

        @pl.loop(i * NX // 4, (i + 1) * NX // 4)
        def _(p):
            two = pl.ds(pl.multiple_of(p * 2 * BLK, 2 * BLK), 2 * BLK)
            part[:, two] = jnp.dot(w2t[...], a_g[:, two], preferred_element_type=F32).astype(BF16)

        start(to_sib[i])

    def products(w_ref, whole):
        @pl.loop(0, NX // 2)
        def _(p):
            two = pl.ds(pl.multiple_of(p * 2 * BLK, 2 * BLK), 2 * BLK)
            prod = jnp.dot(w_ref[...], whole[:, two], preferred_element_type=F32)
            y[pl.ds(p * 2 * K, K)] = prod[:, :BLK].reshape(K, D, BLK)
            y[pl.ds(p * 2 * K + K, K)] = prod[:, BLK:].reshape(K, D, BLK)

    x_all.finish((0, 1, 2, 3))
    products(w1_ref, xall)

    def rows_for(chips):
        return pl.ds(pl.multiple_of(lax.rem(chip + chips, NCHAN // 2) * D, D), D)

    to_ahead = [
        remote(comb.at[rows_for(2), halves[0]], via.at[0], cs.at[0], cr.at[0], (space, ahead)),
        remote(comb.at[rows_for(1), halves[1]], came.at[0, :, halves[1]], cs.at[1], cr.at[1], (space, ahead)),
        remote(comb.at[rows_for(1), halves[0]], came.at[0, :, halves[0]], cs.at[2], cr.at[2], (space, ahead)),
    ]
    to_behind = [
        remote(comb.at[rows_for(2), halves[1]], via.at[1], cs.at[3], cr.at[3], (space, behind)),
        remote(comb.at[rows_for(3), halves[0]], came.at[1, :, halves[0]], cs.at[4], cr.at[4], (space, behind)),
        remote(comb.at[rows_for(3), halves[1]], came.at[1, :, halves[1]], cs.at[5], cr.at[5], (space, behind)),
    ]
    for i, h in enumerate(halves):
        to_sib[i].wait_recv()
        comb[:, h] = (part[ours, h].astype(F32) + sibp[:, h].astype(F32)).astype(BF16)
    for i in range(2):
        start(to_ahead[i])
        start(to_behind[i])

    scan(y, T_ROWS)
    to_ahead[0].wait_recv()
    comb[rows_for(1), halves[0]] = (comb[rows_for(1), halves[0]].astype(F32) + via[0].astype(F32)).astype(BF16)
    start(to_ahead[2])
    to_behind[0].wait_recv()
    comb[rows_for(3), halves[1]] = (comb[rows_for(3), halves[1]].astype(F32) + via[1].astype(F32)).astype(BF16)
    start(to_behind[2])

    for b in range(NB):
        z = run_end(T_TEND, b)
        zblk[b] = z
        h = z / (1.0 + jnp.exp(-z))
        blocks[b] = h
        hall[mine, b * BLK : (b + 1) * BLK] = h.astype(BF16)
    load_last(hlast)
    h_rims = rim_copies(hall, hlast, hrim, qs, qr)
    for copy in h_rims:
        start(copy)
    h_all = Gather(hall, hs, hr)
    h_all.send((0, 1))

    for copy in to_ahead[1:] + to_behind[1:]:
        copy.wait_recv()
    for p in range(0, NX, 4):
        at = pl.ds(p * BLK, 4 * BLK)
        ghown[:, at] = comb[rows_for(0), at].astype(F32) + came[0, :, at].astype(F32) + came[1, :, at].astype(F32)
    back_out[0] = ghown[:, OWN : OWN + RIM]
    back_out[1] = ghown[:, OWN + RIM :]
    n_copies = [
        remote(back_out.at[0], back_in.at[0], ns.at[0], nr.at[0], (left, chan)),
        remote(back_out.at[1], back_in.at[1], ns.at[1], nr.at[1], (right, chan)),
    ]
    for copy in n_copies:
        start(copy)
    for copy in h_rims:
        copy.wait_recv()
    hall[mine, rims] = hrim[...]
    h_all.send((2, 3))
    for copy in n_copies:
        copy.wait_recv()
    for b in range(NB):
        grad = ghown[:, b * BLK : (b + 1) * BLK]
        if b < HB:
            grad = grad + back_in[1, :, b * BLK : (b + 1) * BLK]
        for u in range(HB):
            grad = grad + back_in[0, :, u * BLK : (u + 1) * BLK] * fac[T_LAST + u, b]
        z = zblk[b]
        gate = 1.0 / (1.0 + jnp.exp(-z))
        grad_z = grad * gate * (1.0 + z * (1.0 - gate))
        blocks[b] = grad_z.astype(BF16).astype(F32)
    h_all.relay((0, 1))
    scan(blocks, T_SLOTS)
    h_all.relay((2, 3))
    fill_slots(a_z)

    class Sum:
        def __init__(self, ysend, yrecv, zsend, zrecv, ys, yr, zs, zr):
            self.ysend, self.yrecv, self.zsend, self.zrecv = ysend, yrecv, zsend, zrecv
            self.over_y, self.over_z = [], []
            for i, lanes in enumerate((pl.ds(0, KW), pl.ds(KW, KP - KW))):
                for j in range(1, NY):
                    at = pl.ds(pl.multiple_of(lax.rem(row + j, NY) * CY, CY), CY)
                    n = i * (NY - 1) + j - 1
                    self.over_y.append(
                        remote(ysend.at[at, lanes], yrecv.at[j - 1, :, lanes], ys.at[n], yr.at[n], (along_y(j), chan))
                    )
            for j in range(1, NZ):
                to = lax.rem(col + j, NZ)
                self.over_z.append(
                    remote(zsend.at[to], zrecv.at[j - 1], zs.at[j - 1], zr.at[j - 1], (along_z(j), chan))
                )

        def begin(self, whole, a):
            for n in range(0, KP, 256):
                at = slice(n, min(n + 256, KP))
                self.ysend[:, at] = nt(whole[...], a[at, :]).astype(BF16)
                if at.stop == KW or at.stop == KP:
                    for copy in self.over_y[: NY - 1] if at.stop == KW else self.over_y[NY - 1 :]:
                        start(copy)

        def middle(self):
            for copy in self.over_y:
                copy.wait_recv()
            own = self.ysend[pl.ds(pl.multiple_of(row * CY, CY), CY), :].astype(F32)
            for j in range(NY - 1):
                own = own + self.yrecv[j].astype(F32)
            wide[:, :CH, :] = own[:, :KW].reshape(NZ, CH, KW)
            wide[:, CH:, : KP - KW] = own[:, KW:].reshape(NZ, CH, KP - KW)
            wide[:, CH:, KP - KW :] = jnp.zeros((NZ, CH, 2 * KW - KP), F32)
            self.zsend[...] = wide[...].astype(BF16)
            for copy in self.over_z:
                start(copy)

        def end(self, dst):
            total = self.zsend[col].astype(F32)
            for j, copy in enumerate(self.over_z):
                copy.wait_recv()
                total = total + self.zrecv[j].astype(F32)
            for k in range(K):
                rows, at = (k * D // KW) * CH, k * D % KW
                dst[k] = total[rows : rows + CH, at : at + D]

    one = Sum(ysend1, yrecv1, zsend1, zrecv1, y1s, y1r, z1s, z1r)
    two = Sum(ysend2, yrecv2, zsend2, zrecv2, y2s, y2r, z2s, z2r)
    one.begin(xall, a_z)

    h_all.finish((0, 1, 2, 3))
    two.begin(hall, a_g)
    one.middle()
    products(w2_ref, hall)
    two.middle()
    scan(y, T_ROWS)
    for b in range(NB):
        z = run_end(T_TEND, b)
        out_ref[:, b * BLK : (b + 1) * BLK] = z.astype(BF16)
    one.end(g1_ref)
    two.end(g2_ref)
    for copy in pending:
        copy.wait_send()


def hand_out(*refs):
    for src, dst in zip(refs[:3], refs[3:]):
        dst[...] = src[...]


def local(features, kernel_map, block_count, weight_one, weight_two, cotangent):
    vmem = pl.BlockSpec(memory_space=pltpu.VMEM)
    smem = pl.BlockSpec(memory_space=pltpu.SMEM)
    index, factor = pl.pallas_call(
        tables,
        out_shape=(jax.ShapeDtypeStruct((8, TW), jnp.int32), jax.ShapeDtypeStruct((8, TW), F32)),
        in_specs=[smem, vmem],
        out_specs=(vmem, vmem),
    )(block_count, kernel_map[0].transpose(2, 1, 0))

    def v(shape, kind=BF16):
        return pltpu.VMEM(shape, kind)

    def dma(n):
        return [pltpu.SemaphoreType.DMA((n,))] * 2

    output, one, two = pl.pallas_call(
        kernel,
        out_shape=(
            jax.ShapeDtypeStruct((D, OWN), BF16),
            jax.ShapeDtypeStruct((K, CH, D), F32),
            jax.ShapeDtypeStruct((K, CH, D), F32),
        ),
        in_specs=[smem] * 2 + [vmem] * 4,
        out_specs=(vmem,) * 3,
        scratch_shapes=[
            v((C, EXT)), v((C, EXT)), v((D, RIM)), v((D, 2 * RIM)), v((D, RIM)), v((D, 2 * RIM)),
            v((C, KP)), v((NB, D, BLK), F32), v((NB, D, BLK), F32), v((NSLOT, D, BLK), F32), v((NE, D, BLK), F32),
            v((KP, EXT)), v((KP, EXT)),
            v((C, EXT)), v((C // 2, EXT)), v((C // 2, EXT)), v((2, D, EXT // 2)), v((2, D, EXT)),
            v((D, EXT), F32), v((2, D, RIM), F32), v((2, D, RIM), F32),
            v((C, KP)), v((C, KP)), v((NY - 1, CY, KP)), v((NY - 1, CY, KP)),
            v((NZ, 2 * CH, KW), F32), v((NZ, 2 * CH, KW)), v((NZ, 2 * CH, KW)),
            v((NZ - 1, 2 * CH, KW)), v((NZ - 1, 2 * CH, KW)),
            *dma(28), *dma(2), *dma(28), *dma(2), *dma(2), *dma(6), *dma(2),
            *dma(2 * NY - 2), *dma(2 * NY - 2), *dma(NZ - 1), *dma(NZ - 1),
        ],
        compiler_params=pltpu.CompilerParams(
            collective_id=0, has_side_effects=True, vmem_limit_bytes=56 * 2**20
        ),
    )(
        index,
        factor,
        features.T,
        cotangent.T,
        weight_one.reshape(KD, C),
        weight_two.reshape(KD, C),
    )
    output, one, two = pl.pallas_call(
        hand_out,
        out_shape=tuple(jax.ShapeDtypeStruct(r.shape, r.dtype) for r in (output, one, two)),
        in_specs=[vmem] * 3,
        out_specs=(vmem,) * 3,
    )(output, one, two)
    return output.T, one.transpose(0, 2, 1), two.transpose(0, 2, 1)


def solution(mesh):
    return jax.shard_map(
        local,
        mesh=mesh,
        in_specs=(
            P("space", "chan"),
            P("space", None, None, None),
            P(),
            P(None, "chan", None),
            P(None, "chan", None),
            P("space", "chan"),
        ),
        out_specs=(P("space", "chan"), P(None, "chan", "space"), P(None, "chan", "space")),
        check_vma=False,
    )
```

```python
import jax
import jax.numpy as jnp
from jax import lax
from jax.experimental import pallas as pl
from jax.experimental.pallas import tpu as pltpu
from jax.sharding import PartitionSpec as P

MESH = pl.DeviceIdType.MESH
C = 256
K = 27
BLK = 128
HB = 2
NB = 16
EPK = 16
NX = NB + 2 * HB
NE = K * EPK
NCHAN = 8
NSPACE = 32
D = C // NCHAN
CH = C // NSPACE
KD = K * D
KP = 896
KW = 512
NY = 4
NZ = NSPACE // NY
CY = C // NY
OWN = NB * BLK
RIM = HB * BLK
EXT = NX * BLK
NSLOT = K * NX
F32 = jnp.float32
BF16 = jnp.bfloat16

NP = 512
TW = 640
T_ROWS, T_SLOTS, T_TEND, T_SEND, T_LAST = 0, 1, 2, 3, 4


def nt(a, b):
    return lax.dot_general(a, b, (((1,), (1,)), ((), ())), preferred_element_type=F32)


def by_core():
    row = lax.broadcasted_iota(jnp.int32, (C, C), 0)
    col = lax.broadcasted_iota(jnp.int32, (C, C), 1)
    core, rest = row // (C // 2), row % (C // 2)
    return jnp.where(col == (rest // D) * (2 * D) + core * D + rest % D, 1.0, 0.0).astype(BF16)


def iota(shape, dim):
    return lax.broadcasted_iota(jnp.int32, shape, dim)


def total(cond, axis):
    return jnp.sum(jnp.where(cond, 1.0, 0.0), axis, keepdims=True)


def tables(count_ref, km_ref, index, factor):
    shard = lax.axis_index("space")
    own, left = count_ref[shard], count_ref[jnp.maximum(shard - 1, 0)]
    index[...] = jnp.zeros(index.shape, jnp.int32)
    factor[...] = jnp.zeros(factor.shape, F32)
    shard, own, left = shard.astype(F32), own.astype(F32), left.astype(F32)
    spread = jnp.where((iota((K, NP), 1) & 31) == iota((K, NP), 0), 1.0, 0.0).astype(BF16)
    gather = jnp.where((iota((NP, K), 0) & 31) == iota((NP, K), 1), 1.0, 0.0).astype(BF16)
    at_row = (iota((EPK, NP), 1) >> 5) == iota((EPK, NP), 0)
    at_col = (iota((NP, EPK), 0) >> 5) == iota((NP, EPK), 1)

    def keys(form, axis):
        shape = (1, NP) if axis == 0 else (NP, 1)
        number = iota(shape, 1 - axis)
        offset = number & 31
        source, inblock, target = (form(km_ref[c].astype(BF16)) for c in range(3))
        before = NB + inblock - (left - HB)
        pos = jnp.where(source == shard, inblock, jnp.where(source < shard, before, NB + HB + inblock))
        pos = jnp.clip(pos, 0.0, NX - 1.0)
        target = jnp.clip(target, 0.0, NB - 1.0)
        gone = jnp.maximum(jnp.where(target < own, 0.0, 1.0), jnp.where(offset < K, 0.0, 1.0)) > 0.5
        known = offset < K
        offset = offset.astype(F32)
        by_target = jnp.where(gone, 1.0 * NB, target)
        by_slot = jnp.where(gone, 1.0 * NSLOT, offset * NX + pos)
        product = jnp.where(known, pos * K + offset, 0.0)
        return number.astype(F32), (by_target, by_slot), (product, target)

    def as_row(v):
        wide = jnp.dot(v, spread, preferred_element_type=F32)
        return jnp.sum(jnp.where(at_row, wide, 0.0), 0, keepdims=True)

    def as_col(v):
        return jnp.sum(jnp.where(at_col, nt(gather, v), 0.0), 1, keepdims=True)

    n_row, key_row, _ = keys(as_row, 0)
    n_col, key_col, pay_col = keys(as_col, 1)
    for i, width in enumerate((BLK, TW)):
        key = key_col[i]
        rank = total(key_row[i] * NP + n_row < key * NP + n_col, 1)
        both = jnp.sum(jnp.where(rank == n_row, key * 1024.0 + pay_col[i], 0.0), 0, keepdims=True).astype(jnp.int32)
        sorted_key = (both >> 10).astype(F32)
        index[i : i + 1, :NP] = both & 1023
        factor[i : i + 1, :NP] = jnp.where(total(key < sorted_key, 0) == n_row, 0.0, 1.0)
        at = iota((1, width), 1).astype(F32)
        upto = total(key <= at, 0)
        index[T_TEND + i : T_TEND + i + 1, :width] = jnp.clip(upto - 1.0, 0.0, NE - 1.0).astype(jnp.int32)
        factor[T_TEND + i : T_TEND + i + 1, :width] = jnp.minimum(total(key == at, 0), 1.0)
    block = iota((1, BLK), 1).astype(F32)
    last = jnp.clip(own - HB + block, 0.0, NB - 1.0)
    index[T_LAST : T_LAST + 1, :BLK] = last.astype(jnp.int32)
    for u in range(HB):
        factor[T_LAST + u : T_LAST + u + 1, :BLK] = jnp.where(block == own - HB + u, 1.0, 0.0)


def kernel(
    tab, fac, x_ref, g_ref, w1_ref, w2_ref,
    out_ref, g1_ref, g2_ref,
    xall, hall, xlast, xrim, hlast, hrim, w2t, blocks, zblk, y, run, a_g, a_z,
    part, sibp, comb, via, came, ghown, back_out, back_in,
    ysend1, ysend2, yrecv1, yrecv2, wide, zsend1, zsend2, zrecv1, zrecv2,
    xs, xr, rs, rr, hs, hr, qs, qr, bs, br, cs, cr, ns, nr,
    y1s, y1r, y2s, y2r, z1s, z1r, z2s, z2r,
):
    chan = lax.axis_index("chan")
    space = lax.axis_index("space")
    core = lax.rem(chan, 2)
    chip = chan // 2
    sib = chan + 1 - 2 * core
    ahead = lax.rem(chan + 2, NCHAN)
    behind = lax.rem(chan + NCHAN - 2, NCHAN)
    opposite = lax.rem(chan + NCHAN // 2, NCHAN)
    right = lax.rem(space + 1, NSPACE)
    left = lax.rem(space + NSPACE - 1, NSPACE)
    row = space // NZ
    col = lax.rem(space, NZ)

    def along_y(j):
        return lax.rem(space + j * NZ, NSPACE)

    def along_z(j):
        return row * NZ + lax.rem(col + j, NZ)

    peers = [(space, sib), (space, ahead), (space, behind), (right, chan), (left, chan)]
    peers += [(along_y(j), chan) for j in range(1, NY)] + [(along_z(j), chan) for j in range(1, NZ)]
    barrier = pltpu.get_barrier_semaphore()
    for peer in peers:
        pl.semaphore_signal(barrier, inc=1, device_id=peer, device_id_type=MESH)

    def remote(src, dst, ssem, rsem, device):
        return pltpu.make_async_remote_copy(
            src_ref=src, dst_ref=dst, send_sem=ssem, recv_sem=rsem, device_id=device, device_id_type=MESH
        )

    def channels(who):
        return pl.ds(pl.multiple_of(who * D, D), D)

    mine = channels(chan)
    body = pl.ds(0, OWN)
    rims = pl.ds(OWN, 2 * RIM)
    pending = []

    def start(copy):
        copy.start()
        pending.append(copy)

    class Gather:
        def __init__(self, whole, ssem, rsem):
            half = OWN // 2
            lanes = [pl.ds(0, half), pl.ds(half, half), pl.ds(OWN, RIM), pl.ds(OWN + RIM, RIM)]
            ways = [(chan, ahead), (chan, behind), (chan, sib), None, (behind, sib), (ahead, sib), (opposite, sib)]
            self.copy = {}
            for kind, way in enumerate(ways):
                for p in range(4):
                    origin, to = way or ((behind, ahead), (ahead, behind))[p % 2]
                    ref = whole.at[channels(origin), lanes[p]]
                    n = kind * 4 + p
                    self.copy[kind, p] = remote(ref, ref, ssem.at[n], rsem.at[n], (space, to))

        def send(self, parts):
            for kind in range(3):
                for p in parts:
                    start(self.copy[kind, p])

        def relay(self, parts):
            for p in parts:
                for kind in (0, 1):
                    self.copy[kind, p].wait_recv()
                    if p % 2 == kind:
                        start(self.copy[3, p])
                    start(self.copy[4 + kind, p])

        def finish(self, parts):
            for p in parts:
                self.copy[3, p].wait_recv()
                start(self.copy[6, p])
            for p in parts:
                for kind in (2, 4, 5, 6):
                    self.copy[kind, p].wait_recv()

    def rim_copies(whole, last, rim, ssem, rsem):
        return [
            remote(last, rim.at[:, pl.ds(0, RIM)], ssem.at[0], rsem.at[0], (right, chan)),
            remote(whole.at[mine, pl.ds(0, RIM)], rim.at[:, pl.ds(RIM, RIM)], ssem.at[1], rsem.at[1], (left, chan)),
        ]

    def load_last(last):
        for u in range(HB):
            last[:, u * BLK : (u + 1) * BLK] = blocks[tab[T_LAST, u]].astype(BF16)

    xall[mine, body] = x_ref[...]
    for b in range(NB):
        blocks[b] = x_ref[:, b * BLK : (b + 1) * BLK].astype(F32)
    load_last(xlast)

    pl.semaphore_wait(barrier, len(peers))

    x_rims = rim_copies(xall, xlast, xrim, rs, rr)
    for copy in x_rims:
        start(copy)
    x_all = Gather(xall, xs, xr)
    x_all.send((0, 1))

    def scan(src, base):
        def step(i, total):
            for u in range(8):
                n = i * 8 + u
                total = total * fac[base, n] + src[tab[base, n]]
                run[n] = total
            return total

        lax.fori_loop(0, NE // 8, step, jnp.zeros((D, BLK), F32))

    def run_end(table, at):
        return run[tab[table, at]] * fac[table, at]

    def fill_slots(dst):
        @pl.loop(0, K)
        def _(k):
            at = pl.ds(pl.multiple_of(k * D, D), D)
            for p in range(NX):
                dst[at, p * BLK : (p + 1) * BLK] = run_end(T_SEND, k * NX + p).astype(BF16)

    for b in range(NB):
        blocks[b] = g_ref[:, b * BLK : (b + 1) * BLK].astype(F32)
    a_g[KD:, :] = jnp.zeros((KP - KD, EXT), BF16)
    a_z[KD:, :] = jnp.zeros((KP - KD, EXT), BF16)
    w2t[:, KD:] = jnp.zeros((C, KP - KD), BF16)
    for copy in x_rims:
        copy.wait_recv()
    xall[mine, rims] = xrim[...]
    x_all.send((2, 3))
    w2t[:, :KD] = nt(by_core(), w2_ref[...]).astype(BF16)
    scan(blocks, T_SLOTS)
    x_all.relay((0, 1))
    fill_slots(a_g)
    x_all.relay((2, 3))

    theirs = pl.ds(pl.multiple_of((1 - core) * (C // 2), C // 2), C // 2)
    ours = pl.ds(pl.multiple_of(core * (C // 2), C // 2), C // 2)
    halves = [pl.ds(0, EXT // 2), pl.ds(EXT // 2, EXT // 2)]
    to_sib = [remote(part.at[theirs, h], sibp.at[:, h], bs.at[i], br.at[i], (space, sib)) for i, h in enumerate(halves)]
    for i in range(2):

        @pl.loop(i * NX // 4, (i + 1) * NX // 4)
        def _(p):
            two = pl.ds(pl.multiple_of(p * 2 * BLK, 2 * BLK), 2 * BLK)
            part[:, two] = jnp.dot(w2t[...], a_g[:, two], preferred_element_type=F32).astype(BF16)

        start(to_sib[i])

    def products(w_ref, whole):
        @pl.loop(0, NX // 2)
        def _(p):
            two = pl.ds(pl.multiple_of(p * 2 * BLK, 2 * BLK), 2 * BLK)
            prod = jnp.dot(w_ref[...], whole[:, two], preferred_element_type=F32)
            y[pl.ds(p * 2 * K, K)] = prod[:, :BLK].reshape(K, D, BLK)
            y[pl.ds(p * 2 * K + K, K)] = prod[:, BLK:].reshape(K, D, BLK)

    x_all.finish((0, 1, 2, 3))
    products(w1_ref, xall)

    def rows_for(chips):
        return pl.ds(pl.multiple_of(lax.rem(chip + chips, NCHAN // 2) * D, D), D)

    to_ahead = [
        remote(comb.at[rows_for(2), halves[0]], via.at[0], cs.at[0], cr.at[0], (space, ahead)),
        remote(comb.at[rows_for(1), halves[1]], came.at[0, :, halves[1]], cs.at[1], cr.at[1], (space, ahead)),
        remote(comb.at[rows_for(1), halves[0]], came.at[0, :, halves[0]], cs.at[2], cr.at[2], (space, ahead)),
    ]
    to_behind = [
        remote(comb.at[rows_for(2), halves[1]], via.at[1], cs.at[3], cr.at[3], (space, behind)),
        remote(comb.at[rows_for(3), halves[0]], came.at[1, :, halves[0]], cs.at[4], cr.at[4], (space, behind)),
        remote(comb.at[rows_for(3), halves[1]], came.at[1, :, halves[1]], cs.at[5], cr.at[5], (space, behind)),
    ]
    for i, h in enumerate(halves):
        to_sib[i].wait_recv()
        comb[:, h] = (part[ours, h].astype(F32) + sibp[:, h].astype(F32)).astype(BF16)
    for i in range(2):
        start(to_ahead[i])
        start(to_behind[i])

    scan(y, T_ROWS)
    to_ahead[0].wait_recv()
    comb[rows_for(1), halves[0]] = (comb[rows_for(1), halves[0]].astype(F32) + via[0].astype(F32)).astype(BF16)
    start(to_ahead[2])
    to_behind[0].wait_recv()
    comb[rows_for(3), halves[1]] = (comb[rows_for(3), halves[1]].astype(F32) + via[1].astype(F32)).astype(BF16)
    start(to_behind[2])

    for b in range(NB):
        z = run_end(T_TEND, b)
        zblk[b] = z
        h = z / (1.0 + jnp.exp(-z))
        blocks[b] = h
        hall[mine, b * BLK : (b + 1) * BLK] = h.astype(BF16)
    load_last(hlast)
    h_rims = rim_copies(hall, hlast, hrim, qs, qr)
    for copy in h_rims:
        start(copy)
    h_all = Gather(hall, hs, hr)
    h_all.send((0, 1))

    for copy in to_ahead[1:] + to_behind[1:]:
        copy.wait_recv()
    for p in range(0, NX, 4):
        at = pl.ds(p * BLK, 4 * BLK)
        ghown[:, at] = comb[rows_for(0), at].astype(F32) + came[0, :, at].astype(F32) + came[1, :, at].astype(F32)
    back_out[0] = ghown[:, OWN : OWN + RIM]
    back_out[1] = ghown[:, OWN + RIM :]
    n_copies = [
        remote(back_out.at[0], back_in.at[0], ns.at[0], nr.at[0], (left, chan)),
        remote(back_out.at[1], back_in.at[1], ns.at[1], nr.at[1], (right, chan)),
    ]
    for copy in n_copies:
        start(copy)
    for copy in h_rims:
        copy.wait_recv()
    hall[mine, rims] = hrim[...]
    h_all.send((2, 3))
    for copy in n_copies:
        copy.wait_recv()
    for b in range(NB):
        grad = ghown[:, b * BLK : (b + 1) * BLK]
        if b < HB:
            grad = grad + back_in[1, :, b * BLK : (b + 1) * BLK]
        for u in range(HB):
            grad = grad + back_in[0, :, u * BLK : (u + 1) * BLK] * fac[T_LAST + u, b]
        z = zblk[b]
        gate = 1.0 / (1.0 + jnp.exp(-z))
        grad_z = grad * gate * (1.0 + z * (1.0 - gate))
        blocks[b] = grad_z.astype(BF16).astype(F32)
    h_all.relay((0, 1))
    scan(blocks, T_SLOTS)
    h_all.relay((2, 3))
    fill_slots(a_z)

    class Sum:
        def __init__(self, ysend, yrecv, zsend, zrecv, ys, yr, zs, zr):
            self.ysend, self.yrecv, self.zsend, self.zrecv = ysend, yrecv, zsend, zrecv
            self.over_y, self.over_z = [], []
            for i, lanes in enumerate((pl.ds(0, KW), pl.ds(KW, KP - KW))):
                for j in range(1, NY):
                    at = pl.ds(pl.multiple_of(lax.rem(row + j, NY) * CY, CY), CY)
                    n = i * (NY - 1) + j - 1
                    self.over_y.append(
                        remote(ysend.at[at, lanes], yrecv.at[j - 1, :, lanes], ys.at[n], yr.at[n], (along_y(j), chan))
                    )
            for j in range(1, NZ):
                to = lax.rem(col + j, NZ)
                self.over_z.append(
                    remote(zsend.at[to], zrecv.at[j - 1], zs.at[j - 1], zr.at[j - 1], (along_z(j), chan))
                )

        def begin(self, whole, a):
            for n in range(0, KP, 256):
                at = slice(n, min(n + 256, KP))
                self.ysend[:, at] = nt(whole[...], a[at, :]).astype(BF16)
                if at.stop == KW or at.stop == KP:
                    for copy in self.over_y[: NY - 1] if at.stop == KW else self.over_y[NY - 1 :]:
                        start(copy)

        def middle(self):
            for copy in self.over_y:
                copy.wait_recv()
            own = self.ysend[pl.ds(pl.multiple_of(row * CY, CY), CY), :].astype(F32)
            for j in range(NY - 1):
                own = own + self.yrecv[j].astype(F32)
            wide[:, :CH, :] = own[:, :KW].reshape(NZ, CH, KW)
            wide[:, CH:, : KP - KW] = own[:, KW:].reshape(NZ, CH, KP - KW)
            wide[:, CH:, KP - KW :] = jnp.zeros((NZ, CH, 2 * KW - KP), F32)
            self.zsend[...] = wide[...].astype(BF16)
            for copy in self.over_z:
                start(copy)

        def end(self, dst):
            total = self.zsend[col].astype(F32)
            for j, copy in enumerate(self.over_z):
                copy.wait_recv()
                total = total + self.zrecv[j].astype(F32)
            for k in range(K):
                rows, at = (k * D // KW) * CH, k * D % KW
                dst[k] = total[rows : rows + CH, at : at + D]

    one = Sum(ysend1, yrecv1, zsend1, zrecv1, y1s, y1r, z1s, z1r)
    two = Sum(ysend2, yrecv2, zsend2, zrecv2, y2s, y2r, z2s, z2r)
    one.begin(xall, a_z)

    h_all.finish((0, 1, 2, 3))
    two.begin(hall, a_g)
    one.middle()
    products(w2_ref, hall)
    two.middle()
    scan(y, T_ROWS)
    for b in range(NB):
        z = run_end(T_TEND, b)
        out_ref[:, b * BLK : (b + 1) * BLK] = z.astype(BF16)
    one.end(g1_ref)
    two.end(g2_ref)
    for copy in pending:
        copy.wait_send()


def hand_out(*refs):
    for src, dst in zip(refs[:3], refs[3:]):
        dst[...] = src[...]


def local(features, kernel_map, block_count, weight_one, weight_two, cotangent):
    vmem = pl.BlockSpec(memory_space=pltpu.VMEM)
    smem = pl.BlockSpec(memory_space=pltpu.SMEM)
    index, factor = pl.pallas_call(
        tables,
        out_shape=(jax.ShapeDtypeStruct((8, TW), jnp.int32), jax.ShapeDtypeStruct((8, TW), F32)),
        in_specs=[smem, vmem],
        out_specs=(vmem, vmem),
    )(block_count, kernel_map[0].transpose(2, 1, 0))

    def v(shape, kind=BF16):
        return pltpu.VMEM(shape, kind)

    def dma(n):
        return [pltpu.SemaphoreType.DMA((n,))] * 2

    output, one, two = pl.pallas_call(
        kernel,
        out_shape=(
            jax.ShapeDtypeStruct((D, OWN), BF16),
            jax.ShapeDtypeStruct((K, CH, D), F32),
            jax.ShapeDtypeStruct((K, CH, D), F32),
        ),
        in_specs=[smem] * 2 + [vmem] * 4,
        out_specs=(vmem,) * 3,
        scratch_shapes=[
            v((C, EXT)), v((C, EXT)), v((D, RIM)), v((D, 2 * RIM)), v((D, RIM)), v((D, 2 * RIM)),
            v((C, KP)), v((NB, D, BLK), F32), v((NB, D, BLK), F32), v((NSLOT, D, BLK), F32), v((NE, D, BLK), F32),
            v((KP, EXT)), v((KP, EXT)),
            v((C, EXT)), v((C // 2, EXT)), v((C // 2, EXT)), v((2, D, EXT // 2)), v((2, D, EXT)),
            v((D, EXT), F32), v((2, D, RIM), F32), v((2, D, RIM), F32),
            v((C, KP)), v((C, KP)), v((NY - 1, CY, KP)), v((NY - 1, CY, KP)),
            v((NZ, 2 * CH, KW), F32), v((NZ, 2 * CH, KW)), v((NZ, 2 * CH, KW)),
            v((NZ - 1, 2 * CH, KW)), v((NZ - 1, 2 * CH, KW)),
            *dma(28), *dma(2), *dma(28), *dma(2), *dma(2), *dma(6), *dma(2),
            *dma(2 * NY - 2), *dma(2 * NY - 2), *dma(NZ - 1), *dma(NZ - 1),
        ],
        compiler_params=pltpu.CompilerParams(
            collective_id=0, has_side_effects=True, vmem_limit_bytes=56 * 2**20
        ),
    )(
        index,
        factor,
        features.T,
        cotangent.T,
        weight_one.reshape(KD, C),
        weight_two.reshape(KD, C),
    )
    output, one, two = pl.pallas_call(
        hand_out,
        out_shape=tuple(jax.ShapeDtypeStruct(r.shape, r.dtype) for r in (output, one, two)),
        in_specs=[vmem] * 3,
        out_specs=(vmem,) * 3,
    )(output, one, two)
    return output.T, one.transpose(0, 2, 1), two.transpose(0, 2, 1)


def solution(mesh):
    return jax.shard_map(
        local,
        mesh=mesh,
        in_specs=(
            P("space", "chan"),
            P("space", None, None, None),
            P(),
            P(None, "chan", None),
            P(None, "chan", None),
            P("space", "chan"),
        ),
        out_specs=(P("space", "chan"), P(None, "chan", "space"), P(None, "chan", "space")),
        check_vma=False,
    )
```
